128 devices in a mesh: row: 16 (over z_lo, y, core), col: 8 (over x, z_hi).
Axes of the slice: x: 4, y: 4, z: 4 (z_hi: 2, z_lo: 2; z = z_hi * 2 + z_lo), core: 2. Of those that a mesh axis runs over, the one named last changes fastest.
Arguments:
- queries: bfloat16 [8, 128, 4096], P(None, 'row', 'col'), may hold values from -13 to 13, as said below
- key_cache: bfloat16 [8, 65536, 1024], P(None, ('row', 'col')), may hold values from -13 to 13
- value_cache: bfloat16 [8, 65536, 1024], P(None, ('row', 'col')), may hold values from -6 to 6
- key_table: bfloat16 [1024, 1024], replicated, may hold values from -24 to 24
- value_table: bfloat16 [1024, 1024], replicated, may hold values from -6 to 6
- lengths: int32 [8], replicated, may hold values from 8192 to 65536
- token_ids: int32 [8, 128], P(None, 'row'), may hold values from 0 to 1023
Outputs:
- attended: bfloat16 [8, 128, 4096], P(None, 'row', 'col')
The draws below stay inside these ranges and needn't reach their ends.
Inputs may be any that keep to these rules, and one draw needn't show every extreme that they name: `queries`: entries of the query array lie in the stated range.
All inputs are finite; a program needn't handle non-finite values.
Results may differ from the reference program's by a relative error of at most 0.006.
Values may be sent and summed in bfloat16 or wider, within the bound.
No kernel may reach another device: no remote copies, remote signals or barrier semaphores. Data moves between devices by JAX's collectives and lax.ppermute only.
A program may use at most 192 MiB of HBM per device.

```python
import jax
import jax.numpy as jnp
from jax import lax

USERS = 8
BEAMS = 128
L_DEV = 512
HQ = 32
KH = 8
HD = 128
VOCAB = 1024
CONTEXT = 65536


def anchor_parts(key):
    signs = jnp.where(jax.random.bernoulli(jax.random.fold_in(key, 4242), 0.5, (USERS, KH, HD)), 1.7, -1.7)
    places = jax.random.randint(jax.random.fold_in(key, 4243), (USERS,), 0, CONTEXT // 8 - 1)
    strength = jax.random.uniform(jax.random.fold_in(key, 4244), (USERS,), jnp.float32, 1.5, 4.0)
    return (signs.astype(jnp.float32), places, strength)


def draw_key_cache(key, part):
    base = jnp.clip(jax.random.normal(jax.random.fold_in(key, 11), (USERS, CONTEXT, KH * HD), jnp.float32), -6.0, 6.0)
    anchors, places, strength = anchor_parts(key)
    flat = anchors.reshape(USERS, 1, KH * HD)
    spots = jnp.arange(CONTEXT, dtype=jnp.int32)[None, :, None]
    base = jnp.where(spots == places[:, None, None], 4.0 * flat, base)
    base = jnp.where(spots == places[:, None, None] + 1, 3.96 * flat, base)
    return jnp.clip(base, -13.0, 13.0).astype(jnp.bfloat16)


def draw_queries(key, part):
    base = jnp.clip(jax.random.normal(jax.random.fold_in(key, 21), (USERS, BEAMS, HQ * HD), jnp.float32), -6.0, 6.0)
    anchors, places, strength = anchor_parts(key)
    factor = strength * (81.0 / (11.56 * HD ** 0.5))
    spread = jnp.repeat(anchors, HQ // KH, axis=1).reshape(USERS, 1, HQ * HD) * factor[:, None, None]
    beam_at = jnp.arange(BEAMS, dtype=jnp.int32)[None, :, None]
    base = jnp.where(beam_at == 0, spread, base)
    return jnp.clip(base, -13.0, 13.0).astype(jnp.bfloat16)


def set_ends(entries, rng, least, high):
    extent = entries.shape
    index_at = [jax.random.randint(jax.random.fold_in(rng, axis), (), 0, extent[axis]) for axis in range(len(extent))]
    entries = entries.at[tuple(index_at)].set(least)
    longest = extent.index(max(extent))
    index_at[longest] = (index_at[longest] + 1) % extent[longest]
    return entries.at[tuple(index_at)].set(high)


def levels(key, shape, pieces, least, top_value):
    def one(dim, parts):
        draws = jax.random.uniform(jax.random.fold_in(jax.random.fold_in(key, 6), dim), (parts,), jnp.float32, least / len(pieces), top_value / len(pieces))
        return jnp.repeat(jnp.exp(draws), shape[dim] // parts).reshape((-1,) + (1,) * (len(shape) - dim - 1))

    level = one(*pieces[0])
    for cut in pieces[1:]:
        level = level * one(*cut)
    return level


def noise(own_key, dims, width, reach, shards=(), held_as=jnp.bfloat16):
    level = levels(own_key, dims, shards, -0.22, 0.18) if shards else 1.0
    array = jax.random.normal(own_key, dims, jnp.float32) * width * level
    return jnp.minimum(jnp.maximum(array, -reach), reach).astype(held_as)


def setup_inputs(seed: int = 0) -> dict:
    streams_of = jax.random.split(jax.random.key(seed), 8)
    queries = draw_queries(jax.random.fold_in(streams_of[7], 71), 0)
    key_cache = draw_key_cache(jax.random.fold_in(streams_of[7], 71), 0)
    value_cache = noise(streams_of[2], (USERS, CONTEXT, KH * HD), 1.0, 6.0, ((1, 128),))
    key_table = noise(streams_of[3], (VOCAB, KH * HD), 4.0, 24.0)
    value_table = noise(streams_of[4], (VOCAB, KH * HD), 1.0, 6.0)
    lengths = set_ends(jax.random.randint(streams_of[5], (USERS,), CONTEXT // 8, CONTEXT + 1), jax.random.fold_in(streams_of[5], 1), CONTEXT // 8, CONTEXT).astype(jnp.int32)
    token_ids = set_ends(jax.random.randint(streams_of[6], (USERS, BEAMS), 0, VOCAB), jax.random.fold_in(streams_of[6], 1), 0, VOCAB - 1).astype(jnp.int32)
    return dict(queries=queries, key_cache=key_cache, value_cache=value_cache, key_table=key_table, value_table=value_table, lengths=lengths, token_ids=token_ids)


def reference(queries, key_cache, value_cache, key_table, value_table, lengths, token_ids):
    group = HQ // KH
    scale = HD ** -0.5
    blocks = CONTEXT // L_DEV
    q_all = queries.astype(jnp.float32).reshape(USERS, BEAMS, KH, group, HD)
    own_keys = key_table[token_ids].astype(jnp.float32).reshape(USERS, BEAMS, KH, 1, HD)
    own_values = value_table[token_ids].astype(jnp.float32).reshape(USERS, BEAMS, KH, 1, HD)
    own_scores = jnp.sum(q_all * own_keys, axis=-1) * scale
    starts = jnp.arange(blocks, dtype=jnp.int32) * L_DEV

    def per_user(items):
        q_user, k_user, v_user, limit, self_score, self_value = items
        k_blocks = k_user.reshape(blocks, L_DEV, KH, HD)
        v_blocks = v_user.reshape(blocks, L_DEV, KH, HD)

        def scores(k_blk, start):
            s = jnp.einsum('wkgd,lkd->wkgl', q_user, k_blk.astype(jnp.float32)) * scale
            live = (start + jnp.arange(L_DEV, dtype=jnp.int32)) < limit
            return jnp.where(live, s, -1e30), live

        def pass_max(peak, items):
            k_blk, start = items
            s, live = scores(k_blk, start)
            return jnp.maximum(peak, jnp.max(s, axis=-1)), None

        peak, _ = lax.scan(pass_max, self_score, (k_blocks, starts))
        first = jnp.exp(self_score - peak)

        def pass_sum(carry, items):
            total, numer = carry
            k_blk, v_blk, start = items
            s, live = scores(k_blk, start)
            weight = jnp.where(live, jnp.exp(s - peak[..., None]), 0.0)
            total = total + jnp.sum(weight, axis=-1)
            rounded = weight.astype(jnp.bfloat16).astype(jnp.float32)
            numer = numer + jnp.einsum('wkgl,lkd->wkgd', rounded, v_blk.astype(jnp.float32))
            return (total, numer), None

        init = (first, first[..., None] * self_value)
        (total, numer), _ = lax.scan(pass_sum, init, (k_blocks, v_blocks, starts))
        return (numer / total[..., None]).reshape(BEAMS, HQ * HD).astype(jnp.bfloat16)

    return lax.map(per_user, (q_all, key_cache, value_cache, lengths, own_scores, own_values))
```

```python
import functools

import jax
import jax.numpy as jnp
import numpy as np
from jax import lax
from jax.experimental import pallas as pl
from jax.experimental.pallas import tpu as pltpu
from jax.sharding import Mesh
from jax.sharding import PartitionSpec as P

KH = 8
GROUP = 4
HD = 128
LOG2E = 1.4426950408889634
SCALE = HD**-0.5
FINE = ("zl", "y", "c", "x", "zh")
SIZES = (2, 4, 2, 4, 2)
CHIPS = ("zl", "y", "x", "zh")
DEAD = -(2.0**100)


def partial_kernel(info, q_ref, k0_ref, k1_ref, v0_ref, v1_ref, o_ref):
    users = pl.num_programs(1)
    u = pl.program_id(1)
    length = k0_ref.shape[1]
    rows = GROUP * 16
    at = lax.broadcasted_iota(jnp.int32, (1, length), 1)
    bias0 = jnp.where(at < info[1 + u], 0.0, DEAD)
    bias1 = jnp.where(at < info[1 + users + u], 0.0, DEAD)
    k0 = k0_ref[0]
    k1 = k1_ref[0]
    v0 = v0_ref[0]
    v1 = v1_ref[0]
    lane = lax.broadcasted_iota(jnp.int32, (16, HD), 1)
    per = 2
    dims = (((1,), (1,)), ((), ()))

    @pl.when(u == 0)
    def _():
        o_ref[:, 0, users * rows :, :] = jnp.zeros((o_ref.shape[0], 16, HD), jnp.bfloat16)

    for i in range(0, q_ref.shape[0], per):
        q = q_ref[i : i + per, 0].reshape(per * rows, HD)
        s0 = lax.dot_general(q, k0, dims, preferred_element_type=jnp.float32)
        s1 = lax.dot_general(q, k1, dims, preferred_element_type=jnp.float32)
        s0 = s0 * (SCALE * LOG2E) + bias0
        s1 = s1 * (SCALE * LOG2E) + bias1
        peak = jnp.maximum(
            jnp.max(s0, axis=1, keepdims=True), jnp.max(s1, axis=1, keepdims=True)
        )
        peak = peak.astype(jnp.bfloat16).astype(jnp.float32)
        w0 = jnp.exp2(s0 - peak)
        w1 = jnp.exp2(s1 - peak)
        total = jnp.sum(w0, axis=1, keepdims=True) + jnp.sum(w1, axis=1, keepdims=True)
        numer = jnp.dot(
            w0.astype(jnp.bfloat16), v0, preferred_element_type=jnp.float32
        ) + jnp.dot(w1.astype(jnp.bfloat16), v1, preferred_element_type=jnp.float32)
        numer = (numer * (1.0 / total)).astype(jnp.bfloat16)
        o_ref[i : i + per, 0, pl.ds(pl.multiple_of(u * rows, rows), rows), :] = (
            numer.reshape(per, rows, HD)
        )
        high = total.astype(jnp.bfloat16).astype(jnp.float32)
        low = total - high
        for d in range(per):
            held = o_ref[i + d, 0, users * rows :, :].astype(jnp.float32)
            for g in range(GROUP):
                part = slice(d * rows + g * 16, d * rows + g * 16 + 16)
                base = u * 16 + g
                held = jnp.where(lane == base, peak[part], held)
                held = jnp.where(lane == base + 4, high[part], held)
                held = jnp.where(lane == base + 8, low[part], held)
            o_ref[i + d, 0, users * rows :, :] = held.astype(jnp.bfloat16)


def partials(info, q, k0, k1, v0, v1):
    lead, heads, qrows, _ = q.shape
    rows = GROUP * 16
    users = qrows // rows
    length = k0.shape[1]

    def mine(j, u, info):
        return (info[0] + u, 0, j)

    def other(j, u, info):
        return (u, 0, j)

    cache = (1, length, HD)
    return pl.pallas_call(
        partial_kernel,
        grid_spec=pltpu.PrefetchScalarGridSpec(
            num_scalar_prefetch=1,
            grid=(heads, users),
            in_specs=[
                pl.BlockSpec((lead, 1, rows, HD), lambda j, u, info: (0, j, u, 0)),
                pl.BlockSpec(cache, mine),
                pl.BlockSpec(cache, other),
                pl.BlockSpec(cache, mine),
                pl.BlockSpec(cache, other),
            ],
            out_specs=pl.BlockSpec(
                (lead, 1, qrows + 16, HD), lambda j, u, info: (0, j, 0, 0)
            ),
        ),
        out_shape=jax.ShapeDtypeStruct((lead, heads, qrows + 16, HD), jnp.bfloat16),
        compiler_params=pltpu.CompilerParams(
            dimension_semantics=("arbitrary", "arbitrary"),
            vmem_limit_bytes=40 << 20,
        ),
        cost_estimate=pl.CostEstimate(
            flops=8 * heads * lead * qrows * HD * length,
            bytes_accessed=8 * users * length * heads * HD + 4 * q.size,
            transcendentals=2 * heads * lead * qrows * length,
        ),
    )(info, q, k0, k1, v0, v1)


def combine_kernel(x_ref, own_ref, value_ref, o_ref, w_ref):
    chips = x_ref.shape[0]
    users = value_ref.shape[0]
    rows = GROUP * 16
    base = users * rows
    own = own_ref[...]

    def top(i, peak):
        return jnp.maximum(peak, x_ref[i, base:, :].astype(jnp.float32))

    peak = lax.fori_loop(0, chips, top, own, unroll=8)

    def weigh(i, total):
        held = x_ref[i, base:, :].astype(jnp.float32)
        mass = pltpu.roll(held, HD - 4, 1) + pltpu.roll(held, HD - 8, 1)
        weight = mass * jnp.exp2(held - peak)
        w_ref[i] = weight
        return total + weight

    fresh = jnp.exp2(own - peak)
    total = lax.fori_loop(0, chips, weigh, fresh, unroll=8)
    inverse = 1.0 / total
    fresh = fresh * inverse
    for u in range(users):
        acc = [
            fresh[:, u * 16 + g : u * 16 + g + 1] * value_ref[u] for g in range(GROUP)
        ]

        def add(i, acc):
            weight = w_ref[i] * inverse
            return [
                acc[g]
                + weight[:, u * 16 + g : u * 16 + g + 1]
                * x_ref[i, u * rows + g * 16 : u * rows + g * 16 + 16, :].astype(jnp.float32)
                for g in range(GROUP)
            ]

        acc = lax.fori_loop(0, chips, add, acc, unroll=4)
        for g in range(GROUP):
            o_ref[u, g] = acc[g].astype(jnp.bfloat16)


def combined(x, own, value):
    users = value.shape[0]
    return pl.pallas_call(
        combine_kernel,
        out_shape=jax.ShapeDtypeStruct((users, GROUP, 16, HD), jnp.bfloat16),
        scratch_shapes=[pltpu.VMEM((x.shape[0], 16, HD), jnp.float32)],
        compiler_params=pltpu.CompilerParams(vmem_limit_bytes=40 << 20),
        cost_estimate=pl.CostEstimate(
            flops=2 * x.size, bytes_accessed=2 * x.size, transcendentals=0
        ),
    )(x, own, value)


def body(queries, key_cache, value_cache, key_table, value_table, lengths, token_ids):
    users, beams, _ = queries.shape
    half = users // 2
    length = key_cache.shape[1]
    c = lax.axis_index("c")
    row = (lax.axis_index("zl") * SIZES[1] + lax.axis_index("y")) * 2 + c
    col = lax.axis_index("x") * SIZES[4] + lax.axis_index("zh")
    swap = functools.partial(lax.ppermute, axis_name="c", perm=[(0, 1), (1, 0)])

    def halves(array):
        return (
            lax.dynamic_slice_in_dim(array, c * half, half, 0),
            lax.dynamic_slice_in_dim(array, (1 - c) * half, half, 0),
        )

    q = queries.reshape(users, beams, GROUP, HD).transpose(0, 2, 1, 3)
    q_mine, q_give = halves(q)
    q_chip = jnp.concatenate([q_mine, swap(q_give)], axis=2)
    t_mine, t_give = halves(token_ids)
    tokens = jnp.concatenate([t_mine, swap(t_give)], axis=1)
    k_other = swap(halves(key_cache)[1])
    v_other = swap(halves(value_cache)[1])

    chips = SIZES[0] * SIZES[1] * SIZES[3] * SIZES[4]
    packed = q_chip.reshape(1, half * GROUP * 2 * beams, HD)
    everyone = lax.all_to_all(
        jnp.broadcast_to(packed, (chips, *packed.shape[1:])), CHIPS, 0, 0, tiled=True
    )
    everyone = everyone.reshape(chips // KH, KH, *packed.shape[1:])

    limits = lax.dynamic_slice_in_dim(lengths, c * half, half, 0)
    offset = (row * KH + col) * length
    other = ((row + 1 - 2 * c) * KH + col) * length
    info = jnp.concatenate([(c * half)[None], limits - offset, limits - other]).astype(jnp.int32)
    sent = partials(info, everyone, key_cache, k_other, value_cache, v_other)
    sent = sent.reshape(chips, *sent.shape[2:])
    arrived = lax.all_to_all(sent, CHIPS, 0, 0, tiled=True)

    codes = jnp.arange(key_table.shape[0], dtype=jnp.int32)
    onehot = (tokens[..., None] == codes).astype(jnp.bfloat16)
    keys = lax.dynamic_slice_in_dim(key_table, col * HD, HD, 1)
    values = lax.dynamic_slice_in_dim(value_table, col * HD, HD, 1)
    own_keys = jnp.einsum("uwv,vc->uwc", onehot, keys, preferred_element_type=jnp.float32)
    own_values = jnp.einsum("uwv,vc->uwc", onehot, values, preferred_element_type=jnp.float32)
    own = jnp.sum(q_chip.astype(jnp.float32) * own_keys[:, None], axis=-1) * (SCALE * LOG2E)
    own = jnp.pad(own.transpose(2, 0, 1), ((0, 0), (0, 0), (0, 16 - GROUP)))
    own = jnp.pad(own.reshape(2 * beams, half * 16), ((0, 0), (0, HD - half * 16)))

    result = combined(arrived, own, own_values)
    keep, give = result[:, :, :beams], result[:, :, beams:]
    got = swap(give)
    whole = jnp.where(
        c == 0, jnp.concatenate([keep, got]), jnp.concatenate([got, keep])
    )
    return whole.transpose(0, 2, 1, 3).reshape(users, beams, GROUP * HD)


def solution(mesh):
    fine = Mesh(np.asarray(mesh.devices).reshape(SIZES), FINE)
    row, col = ("zl", "y", "c"), ("x", "zh")
    return jax.shard_map(
        body,
        mesh=fine,
        in_specs=(
            P(None, row, col),
            P(None, row + col, None),
            P(None, row + col, None),
            P(),
            P(),
            P(),
            P(None, row),
        ),
        out_specs=P(None, row, col),
        check_vma=False,
    )
```

```python
import functools

import jax
import jax.numpy as jnp
import numpy as np
from jax import lax
from jax.experimental import pallas as pl
from jax.experimental.pallas import tpu as pltpu
from jax.sharding import Mesh
from jax.sharding import PartitionSpec as P

KH = 8
GROUP = 4
HD = 128
HALF = HD // 2
SCALE2 = HD**-0.5 * 1.4426950408889634
FINE = ("zl", "y", "c", "x", "zh")
SIZES = (2, 4, 2, 4, 2)
CHIPS = ("zl", "y", "x", "zh")
DEAD = -(2.0**100)
ROWS = 64
META = 8
CHUNKS = 2
PARTS = 2


def packed_tiles(first, second):
    low = lax.broadcasted_iota(jnp.int32, (first.shape[0], HD), 1) < ROWS
    out = []
    for k in range(first.shape[1] // HD):
        a = first[:, k * HD : (k + 1) * HD]
        b = second[:, k * HD : (k + 1) * HD]
        crossed = pltpu.roll(jnp.where(low, b, a), ROWS, 1)
        out.append(jnp.where(low, a, crossed))
        out.append(jnp.where(low, crossed, b))
    return out


def partial_kernel(info, q_ref, k0_ref, k1_ref, v0_ref, v1_ref, o_ref, m_ref):
    users = pl.num_programs(0)
    u = pl.program_id(0)
    part = pl.program_id(1)
    length = k0_ref.shape[1]
    leads, heads = q_ref.shape[:2]
    width = leads * ROWS
    limit0 = info[1 + u]
    limit1 = info[1 + users + u]
    rows_dims = (((1,), (1,)), ((), ()))
    first_dims = (((0,), (0,)), ((), ()))

    def run(masked):
        for j in range(heads):
            cols = slice(j * HD, (j + 1) * HD)
            q = q_ref[:, j].reshape(width, HD)
            s0 = lax.dot_general(
                k0_ref[0, :, cols], q, rows_dims, preferred_element_type=jnp.float32
            )
            s1 = lax.dot_general(
                k1_ref[0, :, cols], q, rows_dims, preferred_element_type=jnp.float32
            )
            s0 = s0 * SCALE2
            s1 = s1 * SCALE2
            if masked:
                at = lax.broadcasted_iota(jnp.int32, (length, width), 0)
                s0 = jnp.where(at < limit0, s0, DEAD)
                s1 = jnp.where(at < limit1, s1, DEAD)
            peak = jnp.maximum(
                jnp.max(s0, axis=0, keepdims=True), jnp.max(s1, axis=0, keepdims=True)
            )
            peak = peak.astype(jnp.bfloat16).astype(jnp.float32)
            w0 = jnp.exp2(s0 - peak)
            w1 = jnp.exp2(s1 - peak)
            total = jnp.sum(w0, axis=0, keepdims=True) + jnp.sum(w1, axis=0, keepdims=True)
            numer = lax.dot_general(
                v0_ref[0, :, cols],
                w0.astype(jnp.bfloat16),
                first_dims,
                preferred_element_type=jnp.float32,
            ) + lax.dot_general(
                v1_ref[0, :, cols],
                w1.astype(jnp.bfloat16),
                first_dims,
                preferred_element_type=jnp.float32,
            )
            numer = numer * (1.0 / total)
            spot = pl.ds(pl.multiple_of(u * ROWS, ROWS), ROWS)
            for d, tile in enumerate(packed_tiles(numer[:HALF], numer[HALF:])):
                o_ref[d, part * heads + j, spot, :] = tile.astype(jnp.bfloat16)
            high = total.astype(jnp.bfloat16).astype(jnp.float32)
            low = total - high
            head = part * heads + j
            m_ref[0, head, pl.ds(2 * u, 1), :] = peak
            m_ref[1, head, pl.ds(2 * u, 1), :] = high
            m_ref[0, head, pl.ds(2 * u + 1, 1), :] = low
            m_ref[1, head, pl.ds(2 * u + 1, 1), :] = low

    @pl.when((u == 0) & (part == 0))
    def _():
        m_ref[...] = jnp.zeros_like(m_ref)

    live = (limit0 >= length) & (limit1 >= length)
    pl.when(live)(lambda: run(False))
    pl.when(jnp.logical_not(live))(lambda: run(True))

    @pl.when((u == users - 1) & (part == pl.num_programs(1) - 1))
    def _():
        for j in range(o_ref.shape[1]):
            for d, tile in enumerate(packed_tiles(m_ref[0, j], m_ref[1, j])):
                o_ref[d, j, users * ROWS :, :] = tile.astype(jnp.bfloat16)


def partials(info, q, k0, k1, v0, v1, base):
    lead, heads, qrows, _ = q.shape
    users = qrows // ROWS
    length = k0.shape[1]
    share = heads // PARTS

    def mine(u, p, info):
        return (info[0] + u, 0, p)

    def other(u, p, info):
        return (base + u if base else u, 0, p)

    cache = (1, length, share * HD)
    out = (lead, heads, qrows + META, HD)
    return pl.pallas_call(
        partial_kernel,
        grid_spec=pltpu.PrefetchScalarGridSpec(
            num_scalar_prefetch=1,
            grid=(users, PARTS),
            in_specs=[
                pl.BlockSpec((lead, share, ROWS, HD), lambda u, p, info: (0, p, u, 0)),
                pl.BlockSpec(cache, mine),
                pl.BlockSpec(cache, other),
                pl.BlockSpec(cache, mine),
                pl.BlockSpec(cache, other),
            ],
            out_specs=pl.BlockSpec(out, lambda u, p, info: (0, 0, 0, 0)),
            scratch_shapes=[pltpu.VMEM((2, heads, META, lead * ROWS), jnp.float32)],
        ),
        out_shape=jax.ShapeDtypeStruct(out, jnp.bfloat16),
        compiler_params=pltpu.CompilerParams(
            dimension_semantics=("arbitrary", "arbitrary"),
            vmem_limit_bytes=40 << 20,
        ),
        cost_estimate=pl.CostEstimate(
            flops=8 * heads * lead * qrows * HD * length,
            bytes_accessed=8 * users * length * heads * HD + 4 * q.size,
            transcendentals=2 * heads * lead * qrows * length,
        ),
    )(info, q, k0, k1, v0, v1)


def combine_kernel(x_ref, own_ref, value_ref, o_ref, w_ref):
    chips = x_ref.shape[0]
    users = value_ref.shape[0]
    low = lax.broadcasted_iota(jnp.int32, (1, HD), 1) < ROWS
    for u in range(users):
        own = own_ref[u]

        def stats(i):
            both = x_ref[i, users * ROWS :, :].astype(jnp.float32)
            line = both[2 * u : 2 * u + 1]
            turned = pltpu.roll(line, ROWS, 1)
            return (
                jnp.where(low, line, turned),
                jnp.where(low, turned, line) + both[2 * u + 1 : 2 * u + 2],
            )

        peak = own
        for i in range(chips):
            peak = jnp.maximum(peak, stats(i)[0])
        fresh = jnp.exp2(own - peak)
        total = fresh
        for i in range(chips):
            top, mass = stats(i)
            weight = mass * jnp.exp2(top - peak)
            w_ref[i : i + 1, :] = weight
            total = total + weight
        inverse = 1.0 / total
        acc = value_ref[u] * fresh
        for i in range(chips):
            acc = acc + x_ref[i, u * ROWS : (u + 1) * ROWS, :].astype(jnp.float32) * w_ref[
                i : i + 1, :
            ]
        turned = (acc * inverse).T
        o_ref[u] = jnp.concatenate([turned[:ROWS], turned[ROWS:]], axis=1).astype(
            jnp.bfloat16
        )


def combined(x, own, value):
    users = value.shape[0]
    return pl.pallas_call(
        combine_kernel,
        out_shape=jax.ShapeDtypeStruct((users, ROWS, HD), jnp.bfloat16),
        scratch_shapes=[pltpu.VMEM((x.shape[0], HD), jnp.float32)],
        compiler_params=pltpu.CompilerParams(vmem_limit_bytes=24 << 20),
        cost_estimate=pl.CostEstimate(
            flops=2 * x.size, bytes_accessed=2 * x.size, transcendentals=0
        ),
    )(x, own, value)


def body(queries, key_cache, value_cache, key_table, value_table, lengths, token_ids):
    users, beams, _ = queries.shape
    half = users // 2
    each = half // CHUNKS
    length = key_cache.shape[1]
    c = lax.axis_index("c")
    row = (lax.axis_index("zl") * SIZES[1] + lax.axis_index("y")) * 2 + c
    col = lax.axis_index("x") * SIZES[4] + lax.axis_index("zh")
    swap = functools.partial(lax.ppermute, axis_name="c", perm=[(0, 1), (1, 0)])

    def halves(array):
        return (
            lax.dynamic_slice_in_dim(array, c * half, half, 0),
            lax.dynamic_slice_in_dim(array, (1 - c) * half, half, 0),
        )

    q = queries.reshape(users, beams, GROUP, HD).transpose(0, 2, 1, 3)
    q_mine, q_give = halves(q)
    q_chip = jnp.concatenate([q_mine, swap(q_give)], axis=2)
    chips = SIZES[0] * SIZES[1] * SIZES[3] * SIZES[4]

    everyone = []
    for n in range(CHUNKS):
        packed = q_chip[n * each : (n + 1) * each].reshape(1, each * ROWS, HD)
        got = lax.all_to_all(
            jnp.broadcast_to(packed, (chips, *packed.shape[1:])), CHIPS, 0, 0, tiled=True
        )
        everyone.append(got.reshape(chips // KH, KH, *packed.shape[1:]))

    k_other = swap(halves(key_cache)[1])
    v_other = swap(halves(value_cache)[1])

    limits = lax.dynamic_slice_in_dim(lengths, c * half, half, 0)
    offset = (row * KH + col) * length
    other = ((row + 1 - 2 * c) * KH + col) * length
    arrived = []
    for n in range(CHUNKS):
        part = limits[n * each : (n + 1) * each]
        info = jnp.concatenate(
            [(c * half + n * each)[None], part - offset, part - other]
        ).astype(jnp.int32)
        sent = partials(info, everyone[n], key_cache, k_other, value_cache, v_other, n * each)
        sent = sent.reshape(chips, *sent.shape[2:])
        arrived.append(lax.all_to_all(sent, CHIPS, 0, 0, tiled=True))

    t_mine, t_give = halves(token_ids)
    tokens = jnp.concatenate([t_mine, swap(t_give)], axis=1)
    codes = jnp.arange(key_table.shape[0], dtype=jnp.int32)
    onehot = (tokens[..., None] == codes).astype(jnp.bfloat16)
    keys = lax.dynamic_slice_in_dim(key_table, col * HD, HD, 1)
    values = lax.dynamic_slice_in_dim(value_table, col * HD, HD, 1)
    own_keys = jnp.einsum("uwv,vc->uwc", onehot, keys, preferred_element_type=jnp.float32)
    own_values = jnp.einsum("uwv,vc->uwc", onehot, values, preferred_element_type=jnp.float32)
    own = jnp.sum(q_chip.astype(jnp.float32) * own_keys[:, None], axis=-1) * SCALE2
    own = jnp.tile(own.reshape(half, 1, ROWS), (1, 1, 2))
    own_values = own_values.reshape(half, 2 * beams, 2, HALF).transpose(0, 3, 2, 1)
    own_values = jnp.broadcast_to(
        own_values[:, :, :, None], (half, HALF, 2, GROUP, 2 * beams)
    ).reshape(half, HALF, HD)

    kept, received = [], []
    for n in range(CHUNKS):
        mine = slice(n * each, (n + 1) * each)
        result = combined(arrived[n], own[mine], own_values[mine])
        result = result.reshape(each, GROUP, 2 * beams, HD)
        kept.append(result[:, :, :beams])
        received.append(swap(result[:, :, beams:]))
    whole = jnp.where(
        c == 0, jnp.concatenate(kept + received), jnp.concatenate(received + kept)
    )
    return whole.transpose(0, 2, 1, 3).reshape(users, beams, GROUP * HD)


def solution(mesh):
    fine = Mesh(np.asarray(mesh.devices).reshape(SIZES), FINE)
    row, col = ("zl", "y", "c"), ("x", "zh")
    return jax.shard_map(
        body,
        mesh=fine,
        in_specs=(
            P(None, row, col),
            P(None, row + col, None),
            P(None, row + col, None),
            P(),
            P(),
            P(),
            P(None, row),
        ),
        out_specs=P(None, row, col),
        check_vma=False,
    )
```

```python
import functools

import jax
import jax.numpy as jnp
import numpy as np
from jax import lax
from jax.experimental import pallas as pl
from jax.experimental.pallas import tpu as pltpu
from jax.sharding import Mesh
from jax.sharding import PartitionSpec as P

KH = 8
GROUP = 4
HD = 128
HALF = HD // 2
SCALE2 = HD**-0.5 * 1.4426950408889634
FINE = ("zl", "y", "c", "x", "zh")
SIZES = (2, 4, 2, 4, 2)
CHIPS = ("zl", "y", "x", "zh")
DEAD = -(2.0**100)
ROWS = 64
META = 8
PARTS = 2


def packed_tiles(first, second):
    low = lax.broadcasted_iota(jnp.int32, (first.shape[0], HD), 1) < ROWS
    out = []
    for k in range(first.shape[1] // HD):
        a = first[:, k * HD : (k + 1) * HD]
        b = second[:, k * HD : (k + 1) * HD]
        crossed = pltpu.roll(jnp.where(low, b, a), ROWS, 1)
        out.append(jnp.where(low, a, crossed))
        out.append(jnp.where(low, crossed, b))
    return out


def spread_kernel(holders, q_ref, o_ref):
    for t, w in enumerate(holders):
        o_ref[t] = q_ref[w]


def partial_kernel(
    info, lengths, qa_ref, qb_ref, k0_ref, k1_ref, v0_ref, v1_ref, oa_ref, ob_ref
):
    length = k0_ref.shape[1]
    leads, heads = qa_ref.shape[:2]
    width = 2 * leads * ROWS
    limit0 = lengths[info[0]] - info[2]
    limit1 = lengths[info[0]] - info[3]
    rows_dims = (((1,), (1,)), ((), ()))
    first_dims = (((0,), (0,)), ((), ()))

    def run(masked):
        def head(j):
            if isinstance(j, int):
                cols = slice(j * HD, (j + 1) * HD)
            else:
                cols = pl.ds(pl.multiple_of(j * HD, HD), HD)
            q = jnp.concatenate(
                [
                    qa_ref[:, j].reshape(width // 2, HD),
                    qb_ref[:, j].reshape(width // 2, HD),
                ]
            )
            s0 = lax.dot_general(
                k0_ref[0, :, cols], q, rows_dims, preferred_element_type=jnp.float32
            )
            s1 = lax.dot_general(
                k1_ref[0, :, cols], q, rows_dims, preferred_element_type=jnp.float32
            )
            s0 = s0 * SCALE2
            s1 = s1 * SCALE2
            if masked:
                at = lax.broadcasted_iota(jnp.int32, (length, width), 0)
                s0 = jnp.where(at < limit0, s0, DEAD)
                s1 = jnp.where(at < limit1, s1, DEAD)
            peak = jnp.maximum(
                jnp.max(s0, axis=0, keepdims=True), jnp.max(s1, axis=0, keepdims=True)
            )
            peak = peak.astype(jnp.bfloat16).astype(jnp.float32)
            w0 = jnp.exp2(s0 - peak)
            w1 = jnp.exp2(s1 - peak)
            total = jnp.sum(w0, axis=0, keepdims=True) + jnp.sum(w1, axis=0, keepdims=True)
            numer = lax.dot_general(
                v0_ref[0, :, cols],
                w0.astype(jnp.bfloat16),
                first_dims,
                preferred_element_type=jnp.float32,
            ) + lax.dot_general(
                v1_ref[0, :, cols],
                w1.astype(jnp.bfloat16),
                first_dims,
                preferred_element_type=jnp.float32,
            )
            numer = numer * (1.0 / total)
            high = total.astype(jnp.bfloat16).astype(jnp.float32)
            low = total - high
            top = lax.broadcasted_iota(jnp.int32, (META, width), 0) == 0
            tiles = packed_tiles(numer[:HALF], numer[HALF:])
            notes = packed_tiles(jnp.where(top, peak, low), jnp.where(top, high, low))
            for d in range(2 * leads):
                o_ref = oa_ref if d < leads else ob_ref
                o_ref[d % leads, j, :ROWS, :] = tiles[d].astype(jnp.bfloat16)
                o_ref[d % leads, j, ROWS:, :] = notes[d].astype(jnp.bfloat16)

        if masked:
            pl.loop(0, heads)(head)
        else:
            for j in range(heads):
                head(j)

    live = (limit0 >= length) & (limit1 >= length)
    pl.when(live)(lambda: run(False))
    pl.when(jnp.logical_not(live))(lambda: run(True))


def partials(info, lengths, qa, qb, k0, k1, v0, v1):
    same = qa is qb
    lead, heads = qa.shape[0] // (2 if same else 1), qa.shape[1]
    length = k0.shape[1]
    share = heads // PARTS
    cache = (1, length, share * HD)

    def mine(p, info, lengths):
        return (info[0], 0, p)

    def other(p, info, lengths):
        return (info[1], 0, p)

    def first(p, info, lengths):
        return (0, p, 0, 0)

    def second(p, info, lengths):
        return (1 if same else 0, p, 0, 0)

    out = jax.ShapeDtypeStruct((lead, heads, ROWS + META, HD), jnp.bfloat16)
    block = pl.BlockSpec((lead, share, ROWS + META, HD), first)
    return pl.pallas_call(
        partial_kernel,
        grid_spec=pltpu.PrefetchScalarGridSpec(
            num_scalar_prefetch=2,
            grid=(PARTS,),
            in_specs=[
                pl.BlockSpec((lead, share, ROWS, HD), first),
                pl.BlockSpec((lead, share, ROWS, HD), second),
                pl.BlockSpec(cache, mine),
                pl.BlockSpec(cache, other),
                pl.BlockSpec(cache, mine),
                pl.BlockSpec(cache, other),
            ],
            out_specs=[block, block],
        ),
        out_shape=[out, out],
        compiler_params=pltpu.CompilerParams(
            dimension_semantics=("arbitrary",),
            vmem_limit_bytes=40 << 20,
        ),
        cost_estimate=pl.CostEstimate(
            flops=16 * heads * lead * ROWS * HD * length,
            bytes_accessed=8 * length * heads * HD + 8 * lead * heads * ROWS * HD,
            transcendentals=4 * heads * lead * ROWS * length,
        ),
    )(info, lengths, qa, qb, k0, k1, v0, v1)


def stats_of(notes, low):
    line = notes[:1]
    turned = pltpu.roll(line, ROWS, 1)
    return jnp.where(low, line, turned), jnp.where(low, turned, line) + notes[1:2]


def merge_kernel(*refs):
    o_ref = refs[-1]
    low = lax.broadcasted_iota(jnp.int32, (1, HD), 1) < ROWS
    first = lax.broadcasted_iota(jnp.int32, (META, HD), 0) == 0

    def join(parts):
        def one(t, _):
            pairs = [stats_of(r[t, ROWS:, :].astype(jnp.float32), low) for r in parts]
            peak = functools.reduce(jnp.maximum, [p for p, _ in pairs])
            weights = [m * jnp.exp2(p - peak) for p, m in pairs]
            total = functools.reduce(jnp.add, weights)
            inverse = 1.0 / total
            acc = None
            for r, w in zip(parts, weights):
                term = r[t, :ROWS, :].astype(jnp.float32) * (w * inverse)
                acc = term if acc is None else acc + term
            o_ref[t, :ROWS, :] = acc.astype(jnp.bfloat16)
            high = total.astype(jnp.bfloat16).astype(jnp.float32)
            rest = total - high
            line = jnp.where(low, peak, high)
            o_ref[t, ROWS:, :] = jnp.where(first, line, rest).astype(jnp.bfloat16)
            return 0

        lax.fori_loop(0, parts[0].shape[0], one, 0, unroll=4)

    per = (len(refs) - 1) // 2
    half = pl.num_programs(0) // 2
    pl.when(pl.program_id(0) < half)(lambda: join(refs[:per]))
    pl.when(pl.program_id(0) >= half)(lambda: join(refs[per : 2 * per]))


def merged(left, right):
    count, rows, _ = left[0].shape
    steps = 2
    size = count // steps
    block = (size, rows, HD)
    ahead = pl.BlockSpec(block, lambda i: (jnp.minimum(i, steps - 1), 0, 0))
    behind = pl.BlockSpec(block, lambda i: (jnp.maximum(i - steps, 0), 0, 0))
    return pl.pallas_call(
        merge_kernel,
        grid=(2 * steps,),
        in_specs=[ahead] * len(left) + [behind] * len(right),
        out_specs=pl.BlockSpec(block, lambda i: (i, 0, 0)),
        out_shape=jax.ShapeDtypeStruct((2 * count, rows, HD), jnp.bfloat16),
        compiler_params=pltpu.CompilerParams(
            dimension_semantics=("arbitrary",), vmem_limit_bytes=40 << 20
        ),
        cost_estimate=pl.CostEstimate(
            flops=16 * left[0].size, bytes_accessed=20 * left[0].size, transcendentals=0
        ),
    )(*left, *right)


def combine_kernel(holders, x_ref, own_ref, value_ref, o_ref, w_ref):
    users = value_ref.shape[0]
    low = lax.broadcasted_iota(jnp.int32, (1, HD), 1) < ROWS
    for u in range(users):
        own = own_ref[u]
        senders = [i for i, w in enumerate(holders) if w == u]
        pairs = [stats_of(x_ref[i, ROWS:, :].astype(jnp.float32), low) for i in senders]
        peak = own
        for top, _ in pairs:
            peak = jnp.maximum(peak, top)
        fresh = jnp.exp2(own - peak)
        total = fresh
        for i, (top, mass) in zip(senders, pairs):
            weight = mass * jnp.exp2(top - peak)
            w_ref[i : i + 1, :] = weight
            total = total + weight
        inverse = 1.0 / total
        acc = value_ref[u] * fresh
        for i in senders:
            acc = acc + x_ref[i, :ROWS, :].astype(jnp.float32) * w_ref[i : i + 1, :]
        turned = (acc * inverse).T
        o_ref[u] = jnp.concatenate([turned[:ROWS], turned[ROWS:]], axis=1).astype(
            jnp.bfloat16
        )


def combined(holders, x, own, value):
    users = value.shape[0]
    return pl.pallas_call(
        functools.partial(combine_kernel, holders),
        out_shape=jax.ShapeDtypeStruct((users, ROWS, HD), jnp.bfloat16),
        scratch_shapes=[pltpu.VMEM((x.shape[0], HD), jnp.float32)],
        compiler_params=pltpu.CompilerParams(vmem_limit_bytes=24 << 20),
        cost_estimate=pl.CostEstimate(
            flops=2 * x.size, bytes_accessed=2 * x.size, transcendentals=0
        ),
    )(x, own, value)


def moved(array, axis, step):
    count = SIZES[FINE.index(axis)]
    return lax.ppermute(array, axis, [(i, (i + step) % count) for i in range(count)])


def body(queries, key_cache, value_cache, key_table, value_table, lengths, token_ids):
    users, beams, _ = queries.shape
    half = users // 2
    length = key_cache.shape[1]
    x, y, zl, zh, c = (lax.axis_index(n) for n in ("x", "y", "zl", "zh", "c"))
    row = (zl * SIZES[1] + y) * 2 + c
    col = x * SIZES[4] + zh
    swap = functools.partial(lax.ppermute, axis_name="c", perm=[(0, 1), (1, 0)])

    def halves(array):
        return (
            lax.dynamic_slice_in_dim(array, c * half, half, 0),
            lax.dynamic_slice_in_dim(array, (1 - c) * half, half, 0),
        )

    q = queries.reshape(users, beams, GROUP, HD).transpose(0, 2, 1, 3)
    q_mine, q_give = halves(q)
    q_chip = jnp.concatenate([q_mine, swap(q_give)], axis=2).reshape(half, ROWS, HD)

    holders = [
        (a + b + 2 * h + l) % half
        for l in range(SIZES[0])
        for b in range(SIZES[1])
        for a in range(SIZES[3])
        for h in range(SIZES[4])
    ]
    chips = len(holders)
    held = (x + y + 2 * zh + zl) % half
    operand = pl.pallas_call(
        functools.partial(spread_kernel, holders),
        out_shape=jax.ShapeDtypeStruct((chips, ROWS, HD), jnp.bfloat16),
    )(q_chip)
    got = lax.all_to_all(operand, CHIPS, 0, 0, tiled=True)
    got = got.reshape(chips // KH, KH, ROWS, HD)
    lead = chips // KH // 2
    got_a, got_b = got[:lead], got[lead:]

    k_other = swap(halves(key_cache)[1])
    v_other = swap(halves(value_cache)[1])

    offset = (row * KH + col) * length
    other = ((row + 1 - 2 * c) * KH + col) * length

    def computed(step, qa, qb):
        user = (held - step) % half
        info = jnp.stack([c * half + user, user, offset, other]).astype(jnp.int32)
        return partials(info, lengths, qa, qb, key_cache, k_other, value_cache, v_other)

    left, right = [], []
    for step in (0, 1, -1, 2):
        if step:
            parts = computed(step, moved(got_a, "x", step), moved(got_b, "y", step))
        else:
            parts = computed(0, got, got)
        one, two = (p.reshape(-1, ROWS + META, HD) for p in parts)
        left.append(moved(one, "x", -step) if step else one)
        right.append(moved(two, "y", -step) if step else two)
    arrived = lax.all_to_all(merged(left, right), CHIPS, 0, 0, tiled=True)

    t_mine, t_give = halves(token_ids)
    tokens = jnp.concatenate([t_mine, swap(t_give)], axis=1)
    codes = jnp.arange(key_table.shape[0], dtype=jnp.int32)
    onehot = (tokens[..., None] == codes).astype(jnp.bfloat16)
    keys = lax.dynamic_slice_in_dim(key_table, col * HD, HD, 1)
    values = lax.dynamic_slice_in_dim(value_table, col * HD, HD, 1)
    own_keys = jnp.einsum("uwv,vc->uwc", onehot, keys, preferred_element_type=jnp.float32)
    own_values = jnp.einsum("uwv,vc->uwc", onehot, values, preferred_element_type=jnp.float32)
    q_rows = q_chip.reshape(half, GROUP, 2 * beams, HD).astype(jnp.float32)
    own = jnp.sum(q_rows * own_keys[:, None], axis=-1) * SCALE2
    own = jnp.tile(own.reshape(half, 1, ROWS), (1, 1, 2))
    own_values = own_values.reshape(half, 2 * beams, 2, HALF).transpose(0, 3, 2, 1)
    own_values = jnp.broadcast_to(
        own_values[:, :, :, None], (half, HALF, 2, GROUP, 2 * beams)
    ).reshape(half, HALF, HD)

    result = combined(holders, arrived, own, own_values)
    result = result.reshape(half, GROUP, 2 * beams, HD)
    kept = result[:, :, :beams]
    received = swap(result[:, :, beams:])
    whole = jnp.where(
        c == 0, jnp.concatenate([kept, received]), jnp.concatenate([received, kept])
    )
    return whole.transpose(0, 2, 1, 3).reshape(users, beams, GROUP * HD)


def solution(mesh):
    fine = Mesh(np.asarray(mesh.devices).reshape(SIZES), FINE)
    row, col = ("zl", "y", "c"), ("x", "zh")
    return jax.shard_map(
        body,
        mesh=fine,
        in_specs=(
            P(None, row, col),
            P(None, row + col, None),
            P(None, row + col, None),
            P(),
            P(),
            P(),
            P(None, row),
        ),
        out_specs=P(None, row, col),
        check_vma=False,
    )
```

```python
import functools

import jax
import jax.numpy as jnp
import numpy as np
from jax import lax
from jax.experimental import pallas as pl
from jax.experimental.pallas import tpu as pltpu
from jax.sharding import Mesh
from jax.sharding import PartitionSpec as P

KH = 8
GROUP = 4
HD = 128
HALF = HD // 2
SCALE2 = HD**-0.5 * 1.4426950408889634
FINE = ("zl", "y", "c", "x", "zh")
SIZES = (2, 4, 2, 4, 2)
CHIPS = ("zl", "y", "x", "zh")
DEAD = -(2.0**100)
ROWS = 64
META = 8
PARTS = 4


def packed_tiles(first, second):
    low = lax.broadcasted_iota(jnp.int32, (first.shape[0], HD), 1) < ROWS
    out = []
    for k in range(first.shape[1] // HD):
        a = first[:, k * HD : (k + 1) * HD]
        b = second[:, k * HD : (k + 1) * HD]
        crossed = pltpu.roll(jnp.where(low, b, a), ROWS, 1)
        out.append(jnp.where(low, a, crossed))
        out.append(jnp.where(low, crossed, b))
    return out


def spread_kernel(holders, q_ref, o_ref):
    for t, w in enumerate(holders):
        o_ref[t] = q_ref[w]


def partial_kernel(
    info, lengths, qa_ref, qb_ref, k0_ref, k1_ref, v0_ref, v1_ref, *rest
):
    oa_ref, ob_ref = rest[-2:]
    length = k0_ref.shape[1]
    leads, heads = qa_ref.shape[:2]
    width = 2 * leads * ROWS
    limit0 = lengths[info[0]] - info[2]
    limit1 = lengths[info[0]] - info[3]
    rows_dims = (((1,), (1,)), ((), ()))
    first_dims = (((0,), (0,)), ((), ()))

    def run(masked):
        def head(j):
            if isinstance(j, int):
                cols = slice(j * HD, (j + 1) * HD)
            else:
                cols = pl.ds(pl.multiple_of(j * HD, HD), HD)
            q = jnp.concatenate(
                [
                    qa_ref[:, j].reshape(width // 2, HD),
                    qb_ref[:, j].reshape(width // 2, HD),
                ]
            )
            s0 = lax.dot_general(
                k0_ref[0, :, cols], q, rows_dims, preferred_element_type=jnp.float32
            )
            s1 = lax.dot_general(
                k1_ref[0, :, cols], q, rows_dims, preferred_element_type=jnp.float32
            )
            s0 = s0 * SCALE2
            s1 = s1 * SCALE2
            if masked:
                at = lax.broadcasted_iota(jnp.int32, (length, width), 0)
                s0 = jnp.where(at < limit0, s0, DEAD)
                s1 = jnp.where(at < limit1, s1, DEAD)
            peak = jnp.maximum(
                jnp.max(s0, axis=0, keepdims=True), jnp.max(s1, axis=0, keepdims=True)
            )
            peak = peak.astype(jnp.bfloat16).astype(jnp.float32)
            w0 = jnp.exp2(s0 - peak)
            w1 = jnp.exp2(s1 - peak)
            total = jnp.sum(w0, axis=0, keepdims=True) + jnp.sum(w1, axis=0, keepdims=True)
            numer = lax.dot_general(
                v0_ref[0, :, cols],
                w0.astype(jnp.bfloat16),
                first_dims,
                preferred_element_type=jnp.float32,
            ) + lax.dot_general(
                v1_ref[0, :, cols],
                w1.astype(jnp.bfloat16),
                first_dims,
                preferred_element_type=jnp.float32,
            )
            numer = numer * (1.0 / total)
            high = total.astype(jnp.bfloat16).astype(jnp.float32)
            low = total - high
            top = lax.broadcasted_iota(jnp.int32, (META, width), 0) == 0
            tiles = packed_tiles(numer[:HALF], numer[HALF:])
            notes = packed_tiles(jnp.where(top, peak, low), jnp.where(top, high, low))
            for d in range(2 * leads):
                o_ref = oa_ref if d < leads else ob_ref
                o_ref[d % leads, j, :ROWS, :] = tiles[d].astype(jnp.bfloat16)
                o_ref[d % leads, j, ROWS:, :] = notes[d].astype(jnp.bfloat16)

        if masked:
            pl.loop(0, heads)(head)
        else:
            for j in range(heads):
                head(j)

    live = (limit0 >= length) & (limit1 >= length)
    pl.when(live)(lambda: run(False))
    pl.when(jnp.logical_not(live))(lambda: run(True))


def partials(info, lengths, qa, qb, k0, k1, v0, v1, parts=(0, PARTS), into=()):
    lead, heads = qa.shape[:2]
    length = k0.shape[1]
    share = heads // PARTS
    cache = (1, length, share * HD)
    begin, steps = parts

    def mine(p, info, lengths):
        return (info[0], 0, begin + p)

    def other(p, info, lengths):
        return (info[1], 0, begin + p)

    def heads_at(p, info, lengths):
        return (0, begin + p, 0, 0)

    out = jax.ShapeDtypeStruct((lead, heads, ROWS + META, HD), jnp.bfloat16)
    asked = pl.BlockSpec((lead, share, ROWS, HD), heads_at)
    block = pl.BlockSpec((lead, share, ROWS + META, HD), heads_at)
    return pl.pallas_call(
        partial_kernel,
        grid_spec=pltpu.PrefetchScalarGridSpec(
            num_scalar_prefetch=2,
            grid=(steps,),
            in_specs=[
                asked,
                asked,
                pl.BlockSpec(cache, mine),
                pl.BlockSpec(cache, other),
                pl.BlockSpec(cache, mine),
                pl.BlockSpec(cache, other),
            ]
            + [pl.BlockSpec(memory_space=pl.ANY)] * len(into),
            out_specs=[block, block],
        ),
        out_shape=[out, out],
        input_output_aliases={8 + i: i for i in range(len(into))},
        compiler_params=pltpu.CompilerParams(
            dimension_semantics=("arbitrary",),
            vmem_limit_bytes=60 << 20,
        ),
        cost_estimate=pl.CostEstimate(
            flops=16 * share * steps * lead * ROWS * HD * length,
            bytes_accessed=8 * length * share * steps * HD,
            transcendentals=4 * share * steps * lead * ROWS * length,
        ),
    )(info, lengths, qa, qb, k0, k1, v0, v1, *into)


def stats_of(notes, low):
    line = notes[:1]
    turned = pltpu.roll(line, ROWS, 1)
    return jnp.where(low, line, turned), jnp.where(low, turned, line) + notes[1:2]


def merge_kernel(*refs):
    o_ref = refs[-1]
    low = lax.broadcasted_iota(jnp.int32, (1, HD), 1) < ROWS
    first = lax.broadcasted_iota(jnp.int32, (META, HD), 0) == 0

    def join(parts):
        def one(t, _):
            pairs = [stats_of(r[t, ROWS:, :].astype(jnp.float32), low) for r in parts]
            peak = functools.reduce(jnp.maximum, [p for p, _ in pairs])
            weights = [m * jnp.exp2(p - peak) for p, m in pairs]
            total = functools.reduce(jnp.add, weights)
            inverse = 1.0 / total
            acc = None
            for r, w in zip(parts, weights):
                term = r[t, :ROWS, :].astype(jnp.float32) * (w * inverse)
                acc = term if acc is None else acc + term
            o_ref[t, :ROWS, :] = acc.astype(jnp.bfloat16)
            high = total.astype(jnp.bfloat16).astype(jnp.float32)
            rest = total - high
            line = jnp.where(low, peak, high)
            o_ref[t, ROWS:, :] = jnp.where(first, line, rest).astype(jnp.bfloat16)
            return 0

        lax.fori_loop(0, parts[0].shape[0], one, 0, unroll=4)

    per = (len(refs) - 1) // 2
    half = pl.num_programs(0) // 2
    pl.when(pl.program_id(0) < half)(lambda: join(refs[:per]))
    pl.when(pl.program_id(0) >= half)(lambda: join(refs[per : 2 * per]))


def merged(left, right):
    count, rows, _ = left[0].shape
    steps = 2
    size = count // steps
    block = (size, rows, HD)
    ahead = pl.BlockSpec(block, lambda i: (jnp.minimum(i, steps - 1), 0, 0))
    behind = pl.BlockSpec(block, lambda i: (jnp.maximum(i - steps, 0), 0, 0))
    return pl.pallas_call(
        merge_kernel,
        grid=(2 * steps,),
        in_specs=[ahead] * len(left) + [behind] * len(right),
        out_specs=pl.BlockSpec(block, lambda i: (i, 0, 0)),
        out_shape=jax.ShapeDtypeStruct((2 * count, rows, HD), jnp.bfloat16),
        compiler_params=pltpu.CompilerParams(
            dimension_semantics=("arbitrary",), vmem_limit_bytes=60 << 20
        ),
        cost_estimate=pl.CostEstimate(
            flops=16 * left[0].size, bytes_accessed=20 * left[0].size, transcendentals=0
        ),
    )(*left, *right)


def combine_kernel(holders, x_ref, own_ref, value_ref, o_ref, w_ref):
    users = value_ref.shape[0]
    low = lax.broadcasted_iota(jnp.int32, (1, HD), 1) < ROWS
    for u in range(users):
        own = own_ref[u]
        senders = [i for i, w in enumerate(holders) if w == u]
        pairs = [stats_of(x_ref[i, ROWS:, :].astype(jnp.float32), low) for i in senders]
        peak = own
        for top, _ in pairs:
            peak = jnp.maximum(peak, top)
        fresh = jnp.exp2(own - peak)
        total = fresh
        for i, (top, mass) in zip(senders, pairs):
            weight = mass * jnp.exp2(top - peak)
            w_ref[i : i + 1, :] = weight
            total = total + weight
        inverse = 1.0 / total
        acc = value_ref[u] * fresh
        for i in senders:
            acc = acc + x_ref[i, :ROWS, :].astype(jnp.float32) * w_ref[i : i + 1, :]
        turned = (acc * inverse).T
        o_ref[u] = jnp.concatenate([turned[:ROWS], turned[ROWS:]], axis=1).astype(
            jnp.bfloat16
        )


def combined(holders, x, own, value):
    users = value.shape[0]
    return pl.pallas_call(
        functools.partial(combine_kernel, holders),
        out_shape=jax.ShapeDtypeStruct((users, ROWS, HD), jnp.bfloat16),
        scratch_shapes=[pltpu.VMEM((x.shape[0], HD), jnp.float32)],
        compiler_params=pltpu.CompilerParams(vmem_limit_bytes=24 << 20),
        cost_estimate=pl.CostEstimate(
            flops=2 * x.size, bytes_accessed=2 * x.size, transcendentals=0
        ),
    )(x, own, value)


def moved(array, axis, step):
    count = SIZES[FINE.index(axis)]
    return lax.ppermute(array, axis, [(i, (i + step) % count) for i in range(count)])


def body(queries, key_cache, value_cache, key_table, value_table, lengths, token_ids):
    users, beams, _ = queries.shape
    half = users // 2
    length = key_cache.shape[1]
    x, y, zl, zh, c = (lax.axis_index(n) for n in ("x", "y", "zl", "zh", "c"))
    row = (zl * SIZES[1] + y) * 2 + c
    col = x * SIZES[4] + zh
    swap = functools.partial(lax.ppermute, axis_name="c", perm=[(0, 1), (1, 0)])

    def halves(array):
        return (
            lax.dynamic_slice_in_dim(array, c * half, half, 0),
            lax.dynamic_slice_in_dim(array, (1 - c) * half, half, 0),
        )

    q = queries.reshape(users, beams, GROUP, HD).transpose(0, 2, 1, 3)
    q_mine, q_give = halves(q)
    t_mine, t_give = halves(token_ids)
    q_give, t_give, key_source = lax.optimization_barrier((q_give, t_give, key_cache))
    q_chip = jnp.concatenate([q_mine, swap(q_give)], axis=2).reshape(half, ROWS, HD)
    tokens = jnp.concatenate([t_mine, swap(t_give)], axis=1)

    holders = [
        (a + b + 2 * h + l) % half
        for l in range(SIZES[0])
        for b in range(SIZES[1])
        for a in range(SIZES[3])
        for h in range(SIZES[4])
    ]
    chips = len(holders)
    held = (x + y + 2 * zh + zl) % half
    operand = pl.pallas_call(
        functools.partial(spread_kernel, holders),
        out_shape=jax.ShapeDtypeStruct((chips, ROWS, HD), jnp.bfloat16),
        compiler_params=pltpu.CompilerParams(vmem_limit_bytes=60 << 20),
    )(q_chip)
    operand, value_source = lax.optimization_barrier((operand, value_cache))
    got = lax.all_to_all(operand, CHIPS, 0, 0, tiled=True)
    got = got.reshape(chips // KH, KH, ROWS, HD)
    lead = chips // KH // 2
    got_a, got_b = got[:lead], got[lead:]

    k_other = swap(halves(key_source)[1])
    v_other = swap(halves(value_source)[1])
    got_a, got_b, k_other, v_other = lax.optimization_barrier(
        (got_a, got_b, k_other, v_other)
    )

    offset = (row * KH + col) * length
    other = ((row + 1 - 2 * c) * KH + col) * length

    def computed(step, qa, qb, **kept):
        user = (held - step) % half
        info = jnp.stack([c * half + user, user, offset, other]).astype(jnp.int32)
        return partials(
            info, lengths, qa, qb, key_cache, k_other, value_cache, v_other, **kept
        )

    def flat(parts):
        return [p.reshape(-1, ROWS + META, HD) for p in parts]

    near = [(moved(got_a, "x", s), moved(got_b, "y", s)) for s in (1, -1)]
    begun = computed(0, got_a, got_b, parts=(0, PARTS // 2))
    near, begun, far_a, far_b = lax.optimization_barrier((near, begun, got_a, got_b))
    asked = {1: near[0], -1: near[1], 2: (moved(far_a, "x", 2), moved(far_b, "y", 2))}
    left, right = [], []
    for step, (qa, qb) in asked.items():
        parts = computed(step, qa, qb)
        one, two = flat(parts)
        left.append(moved(one, "x", -step))
        right.append(moved(two, "y", -step))
    begun, _ = lax.optimization_barrier((begun, parts))
    one, two = flat(
        computed(0, got_a, got_b, parts=(PARTS // 2, PARTS - PARTS // 2), into=begun)
    )
    left.append(one)
    right.append(two)
    arrived = lax.all_to_all(merged(left, right), CHIPS, 0, 0, tiled=True)

    codes = jnp.arange(key_table.shape[0], dtype=jnp.int32)
    onehot = (tokens[..., None] == codes).astype(jnp.bfloat16)
    keys = lax.dynamic_slice_in_dim(key_table, col * HD, HD, 1)
    values = lax.dynamic_slice_in_dim(value_table, col * HD, HD, 1)
    own_keys = jnp.einsum("uwv,vc->uwc", onehot, keys, preferred_element_type=jnp.float32)
    own_values = jnp.einsum("uwv,vc->uwc", onehot, values, preferred_element_type=jnp.float32)
    q_rows = q_chip.reshape(half, GROUP, 2 * beams, HD).astype(jnp.float32)
    own = jnp.sum(q_rows * own_keys[:, None], axis=-1) * SCALE2
    own = jnp.tile(own.reshape(half, 1, ROWS), (1, 1, 2))
    own_values = own_values.reshape(half, 2 * beams, 2, HALF).transpose(0, 3, 2, 1)
    own_values = jnp.broadcast_to(
        own_values[:, :, :, None], (half, HALF, 2, GROUP, 2 * beams)
    ).reshape(half, HALF, HD)

    result = combined(holders, arrived, own, own_values)
    result = result.reshape(half, GROUP, 2 * beams, HD)
    kept = result[:, :, :beams]
    received = swap(result[:, :, beams:])
    whole = jnp.where(
        c == 0, jnp.concatenate([kept, received]), jnp.concatenate([received, kept])
    )
    return whole.transpose(0, 2, 1, 3).reshape(users, beams, GROUP * HD)


def solution(mesh):
    fine = Mesh(np.asarray(mesh.devices).reshape(SIZES), FINE)
    row, col = ("zl", "y", "c"), ("x", "zh")
    return jax.shard_map(
        body,
        mesh=fine,
        in_specs=(
            P(None, row, col),
            P(None, row + col, None),
            P(None, row + col, None),
            P(),
            P(),
            P(),
            P(None, row),
        ),
        out_specs=P(None, row, col),
        check_vma=False,
    )
```

```python
import functools

import jax
import jax.numpy as jnp
import numpy as np
from jax import lax
from jax.experimental import pallas as pl
from jax.experimental.pallas import tpu as pltpu
from jax.sharding import Mesh
from jax.sharding import PartitionSpec as P

KH = 8
GROUP = 4
HD = 128
HALF = HD // 2
SCALE2 = HD**-0.5 * 1.4426950408889634
FINE = ("zl", "y", "c", "x", "zh")
SIZES = (2, 4, 2, 4, 2)
CHIPS = ("zl", "y", "x", "zh")
DEAD = -(2.0**100)
ROWS = 64
META = 8
PARTS = 2


def packed_tiles(first, second):
    low = lax.broadcasted_iota(jnp.int32, (first.shape[0], HD), 1) < ROWS
    out = []
    for k in range(first.shape[1] // HD):
        a = first[:, k * HD : (k + 1) * HD]
        b = second[:, k * HD : (k + 1) * HD]
        crossed = pltpu.roll(jnp.where(low, b, a), ROWS, 1)
        out.append(jnp.where(low, a, crossed))
        out.append(jnp.where(low, crossed, b))
    return out


def partial_kernel(
    step, info, lengths, qa_ref, qb_ref, k0_ref, k1_ref, v0_ref, v1_ref, *rest
):
    oa_ref, ob_ref = rest[-2:]
    length = k0_ref.shape[1]
    leads, heads = qa_ref.shape[:2]
    width = 2 * leads * ROWS
    user = (info[1] + (KH - step)) % (lengths.shape[0] // 2)
    limit0 = lengths[info[0] + user] - info[2]
    limit1 = lengths[info[0] + user] - info[3]
    limits = (limit0, limit1)
    rows_dims = (((1,), (1,)), ((), ()))
    first_dims = (((0,), (0,)), ((), ()))

    def columns(j):
        if isinstance(j, int):
            return slice(j * HD, (j + 1) * HD)
        return pl.ds(pl.multiple_of(j * HD, HD), HD)

    def scores(j):
        cols = columns(j)
        q = jnp.concatenate(
            [
                qa_ref[:, j].reshape(width // 2, HD),
                qb_ref[:, j].reshape(width // 2, HD),
            ]
        )
        return [
            lax.dot_general(k[0, :, cols], q, rows_dims, preferred_element_type=jnp.float32)
            for k in (k0_ref, k1_ref)
        ]

    def weights(s, masked):
        s = [part * SCALE2 for part in s]
        if masked:
            at = lax.broadcasted_iota(jnp.int32, (length, width), 0)
            s = [jnp.where(at < limit, part, DEAD) for limit, part in zip(limits, s)]
        peak = jnp.maximum(*[jnp.max(part, axis=0, keepdims=True) for part in s])
        peak = peak.astype(jnp.bfloat16).astype(jnp.float32)
        w = [jnp.exp2(part - peak) for part in s]
        total = sum(jnp.sum(part, axis=0, keepdims=True) for part in w)
        return [part.astype(jnp.bfloat16) for part in w], total, peak

    def store(j, w, total, peak):
        cols = columns(j)
        numer = sum(
            lax.dot_general(
                v[0, :, cols], part, first_dims, preferred_element_type=jnp.float32
            )
            for v, part in zip((v0_ref, v1_ref), w)
        )
        numer = numer * (1.0 / total)
        high = total.astype(jnp.bfloat16).astype(jnp.float32)
        low = total - high
        top = lax.broadcasted_iota(jnp.int32, (META, width), 0) == 0
        tiles = packed_tiles(numer[:HALF], numer[HALF:])
        notes = packed_tiles(jnp.where(top, peak, low), jnp.where(top, high, low))
        for d in range(2 * leads):
            o_ref = oa_ref if d < leads else ob_ref
            o_ref[d % leads, j, :ROWS, :] = tiles[d].astype(jnp.bfloat16)
            o_ref[d % leads, j, ROWS:, :] = notes[d].astype(jnp.bfloat16)

    live = (limit0 >= length) & (limit1 >= length)

    @pl.when(live)
    def _():
        s = scores(0)
        for j in range(heads):
            ahead = scores(j + 1) if j + 1 < heads else None
            store(j, *weights(s, False))
            s = ahead

    @pl.when(jnp.logical_not(live))
    def _():
        @pl.loop(0, heads)
        def _(j):
            store(j, *weights(scores(j), True))


def partials(step, info, lengths, qa, qb, k0, k1, v0, v1, parts=(0, PARTS), into=()):
    lead, heads = qa.shape[:2]
    length = k0.shape[1]
    share = heads // PARTS
    cache = (1, length, share * HD)
    begin, steps = parts
    half = lengths.shape[0] // 2

    def mine(p, info, lengths):
        return (info[0] + (info[1] + (KH - step)) % half, 0, begin + p)

    def other(p, info, lengths):
        return ((info[1] + (KH - step)) % half, 0, begin + p)

    def heads_at(p, info, lengths):
        return (0, begin + p, 0, 0)

    out = jax.ShapeDtypeStruct((lead, heads, ROWS + META, HD), jnp.bfloat16)
    asked = pl.BlockSpec((lead, share, ROWS, HD), heads_at)
    block = pl.BlockSpec((lead, share, ROWS + META, HD), heads_at)
    return pl.pallas_call(
        functools.partial(partial_kernel, step),
        grid_spec=pltpu.PrefetchScalarGridSpec(
            num_scalar_prefetch=2,
            grid=(steps,),
            in_specs=[
                asked,
                asked,
                pl.BlockSpec(cache, mine),
                pl.BlockSpec(cache, other),
                pl.BlockSpec(cache, mine),
                pl.BlockSpec(cache, other),
            ]
            + [pl.BlockSpec(memory_space=pl.ANY)] * len(into),
            out_specs=[block, block],
        ),
        out_shape=[out, out],
        input_output_aliases={8 + i: i for i in range(len(into))},
        compiler_params=pltpu.CompilerParams(
            dimension_semantics=("arbitrary",),
            vmem_limit_bytes=60 << 20,
        ),
        cost_estimate=pl.CostEstimate(
            flops=16 * share * steps * lead * ROWS * HD * length,
            bytes_accessed=8 * length * share * steps * HD,
            transcendentals=4 * share * steps * lead * ROWS * length,
        ),
    )(info, lengths, qa, qb, k0, k1, v0, v1, *into)


def stats_of(notes, low):
    line = notes[:1]
    turned = pltpu.roll(line, ROWS, 1)
    return jnp.where(low, line, turned), jnp.where(low, turned, line) + notes[1:2]


def merge_kernel(*refs):
    o_ref = refs[-1]
    low = lax.broadcasted_iota(jnp.int32, (1, HD), 1) < ROWS
    first = lax.broadcasted_iota(jnp.int32, (META, HD), 0) == 0

    def join(parts):
        def one(t, _):
            pairs = [stats_of(r[t, ROWS:, :].astype(jnp.float32), low) for r in parts]
            peak = functools.reduce(jnp.maximum, [p for p, _ in pairs])
            weights = [m * jnp.exp2(p - peak) for p, m in pairs]
            total = functools.reduce(jnp.add, weights)
            inverse = 1.0 / total
            acc = None
            for r, w in zip(parts, weights):
                term = r[t, :ROWS, :].astype(jnp.float32) * (w * inverse)
                acc = term if acc is None else acc + term
            o_ref[t, :ROWS, :] = acc.astype(jnp.bfloat16)
            high = total.astype(jnp.bfloat16).astype(jnp.float32)
            rest = total - high
            line = jnp.where(low, peak, high)
            o_ref[t, ROWS:, :] = jnp.where(first, line, rest).astype(jnp.bfloat16)
            return 0

        lax.fori_loop(0, parts[0].shape[0], one, 0, unroll=8)

    per = (len(refs) - 1) // 2
    pl.when(pl.program_id(0) == 0)(lambda: join(refs[:per]))
    pl.when(pl.program_id(0) == 1)(lambda: join(refs[per : 2 * per]))


def merged(left, right):
    count, rows, _ = left[0].shape
    vmem = pl.BlockSpec(memory_space=pltpu.VMEM)
    return pl.pallas_call(
        merge_kernel,
        grid=(2,),
        in_specs=[vmem] * (len(left) + len(right)),
        out_specs=pl.BlockSpec((count, rows, HD), lambda i: (i, 0, 0)),
        out_shape=jax.ShapeDtypeStruct((2 * count, rows, HD), jnp.bfloat16),
        compiler_params=pltpu.CompilerParams(dimension_semantics=("arbitrary",), vmem_limit_bytes=52 << 20),
        cost_estimate=pl.CostEstimate(
            flops=16 * left[0].size, bytes_accessed=20 * left[0].size, transcendentals=0
        ),
    )(*left, *right)


def combine_kernel(holders, x_ref, own_ref, value_ref, o_ref, w_ref):
    users = value_ref.shape[0]
    low = lax.broadcasted_iota(jnp.int32, (1, HD), 1) < ROWS
    for u in range(users):
        own = own_ref[u]
        senders = [i for i, w in enumerate(holders) if w == u]
        pairs = [stats_of(x_ref[i, ROWS:, :].astype(jnp.float32), low) for i in senders]
        peak = own
        for top, _ in pairs:
            peak = jnp.maximum(peak, top)
        fresh = jnp.exp2(own - peak)
        total = fresh
        for i, (top, mass) in zip(senders, pairs):
            weight = mass * jnp.exp2(top - peak)
            w_ref[i : i + 1, :] = weight
            total = total + weight
        inverse = 1.0 / total
        acc = value_ref[u] * fresh
        for i in senders:
            acc = acc + x_ref[i, :ROWS, :].astype(jnp.float32) * w_ref[i : i + 1, :]
        turned = (acc * inverse).T
        o_ref[u] = jnp.concatenate([turned[:ROWS], turned[ROWS:]], axis=1).astype(
            jnp.bfloat16
        )


def combined(holders, x, own, value):
    users = value.shape[0]
    return pl.pallas_call(
        functools.partial(combine_kernel, holders),
        out_shape=jax.ShapeDtypeStruct((users, ROWS, HD), jnp.bfloat16),
        scratch_shapes=[pltpu.VMEM((x.shape[0], HD), jnp.float32)],
        compiler_params=pltpu.CompilerParams(vmem_limit_bytes=24 << 20),
        cost_estimate=pl.CostEstimate(
            flops=2 * x.size, bytes_accessed=2 * x.size, transcendentals=0
        ),
    )(x, own, value)


def moved(array, axis, step):
    count = SIZES[FINE.index(axis)]
    return lax.ppermute(array, axis, [(i, (i + step) % count) for i in range(count)])


def body(queries, key_cache, value_cache, key_table, value_table, lengths, token_ids):
    users, beams, _ = queries.shape
    half = users // 2
    length = key_cache.shape[1]
    x, y, zl, zh, c = (lax.axis_index(n) for n in ("x", "y", "zl", "zh", "c"))
    row = (zl * SIZES[1] + y) * 2 + c
    col = x * SIZES[4] + zh
    swap = functools.partial(lax.ppermute, axis_name="c", perm=[(0, 1), (1, 0)])

    def halves(array):
        return (
            lax.dynamic_slice_in_dim(array, c * half, half, 0),
            lax.dynamic_slice_in_dim(array, (1 - c) * half, half, 0),
        )

    q = queries.reshape(users, beams, GROUP, HD).transpose(0, 2, 1, 3)
    q_mine, q_give = halves(q)
    t_mine, t_give = halves(token_ids)
    q_give, t_give, key_source = lax.optimization_barrier((q_give, t_give, key_cache))
    q_chip = jnp.concatenate([q_mine, swap(q_give)], axis=2).reshape(half, ROWS, HD)
    tokens = jnp.concatenate([t_mine, swap(t_give)], axis=1)

    holders = [
        (a + b + 2 * h + l) % half
        for l in range(SIZES[0])
        for b in range(SIZES[1])
        for a in range(SIZES[3])
        for h in range(SIZES[4])
    ]
    chips = len(holders)
    held = (x + y + 2 * zh + zl) % half
    marks = np.asarray(holders).reshape(chips, 1, 1)
    operand = jnp.broadcast_to(q_chip[0], (chips, ROWS, HD))
    for w in range(1, half):
        operand = jnp.where(marks == w, q_chip[w], operand)
    operand, value_source = lax.optimization_barrier((operand, value_cache))
    got = lax.all_to_all(operand, CHIPS, 0, 0, tiled=True)
    got = got.reshape(chips // KH, KH, ROWS, HD)
    lead = chips // KH // 2
    got_a, got_b = got[:lead], got[lead:]

    k_other = swap(halves(key_source)[1])
    v_other = swap(halves(value_source)[1])
    got_a, got_b, k_other, v_other = lax.optimization_barrier(
        (got_a, got_b, k_other, v_other)
    )

    offset = (row * KH + col) * length
    other = ((row + 1 - 2 * c) * KH + col) * length

    info = jnp.stack([c * half, held, offset, other]).astype(jnp.int32)

    def computed(step, qa, qb, **kept):
        return partials(
            step, info, lengths, qa, qb, key_cache, k_other, value_cache, v_other, **kept
        )

    def flat(parts):
        return [p.reshape(-1, ROWS + META, HD) for p in parts]

    near = [(moved(got_a, "x", s), moved(got_b, "y", s)) for s in (1, -1)]
    begun = computed(0, got_a, got_b, parts=(0, PARTS // 2))
    near, begun, far_a, far_b = lax.optimization_barrier((near, begun, got_a, got_b))
    asked = {1: near[0], -1: near[1], 2: (moved(far_a, "x", 2), moved(far_b, "y", 2))}
    left, right = [], []
    for step, (qa, qb) in asked.items():
        parts = computed(step, qa, qb)
        one, two = flat(parts)
        left.append(moved(one, "x", -step))
        right.append(moved(two, "y", -step))
    begun, _ = lax.optimization_barrier((begun, parts))
    one, two = flat(
        computed(0, got_a, got_b, parts=(PARTS // 2, PARTS - PARTS // 2), into=begun)
    )
    left.append(one)
    right.append(two)
    arrived = lax.all_to_all(merged(left, right), CHIPS, 0, 0, tiled=True)

    codes = jnp.arange(key_table.shape[0], dtype=jnp.int32)
    onehot = (tokens[..., None] == codes).astype(jnp.bfloat16)
    keys = lax.dynamic_slice_in_dim(key_table, col * HD, HD, 1)
    values = lax.dynamic_slice_in_dim(value_table, col * HD, HD, 1)
    own_keys = jnp.einsum("uwv,vc->uwc", onehot, keys, preferred_element_type=jnp.float32)
    own_values = jnp.einsum("uwv,vc->uwc", onehot, values, preferred_element_type=jnp.float32)
    q_rows = q_chip.reshape(half, GROUP, 2 * beams, HD).astype(jnp.float32)
    own = jnp.sum(q_rows * own_keys[:, None], axis=-1) * SCALE2
    own = jnp.tile(own.reshape(half, 1, ROWS), (1, 1, 2))
    own_values = own_values.reshape(half, 2 * beams, 2, HALF).transpose(0, 3, 2, 1)
    own_values = jnp.broadcast_to(
        own_values[:, :, :, None], (half, HALF, 2, GROUP, 2 * beams)
    ).reshape(half, HALF, HD)

    result = combined(holders, arrived, own, own_values)
    result = result.reshape(half, GROUP, 2 * beams, HD)
    kept = result[:, :, :beams]
    received = swap(result[:, :, beams:])
    whole = jnp.where(
        c == 0, jnp.concatenate([kept, received]), jnp.concatenate([received, kept])
    )
    return whole.transpose(0, 2, 1, 3).reshape(users, beams, GROUP * HD)


def solution(mesh):
    fine = Mesh(np.asarray(mesh.devices).reshape(SIZES), FINE)
    row, col = ("zl", "y", "c"), ("x", "zh")
    return jax.shard_map(
        body,
        mesh=fine,
        in_specs=(
            P(None, row, col),
            P(None, row + col, None),
            P(None, row + col, None),
            P(),
            P(),
            P(),
            P(None, row),
        ),
        out_specs=P(None, row, col),
        check_vma=False,
    )
```

```python
import functools

import jax
import jax.numpy as jnp
import numpy as np
from jax import lax
from jax.experimental import pallas as pl
from jax.experimental.pallas import tpu as pltpu
from jax.sharding import Mesh
from jax.sharding import PartitionSpec as P

KH = 8
GROUP = 4
HD = 128
HALF = HD // 2
SCALE2 = HD**-0.5 * 1.4426950408889634
FINE = ("zl", "y", "c", "x", "zh")
SIZES = (2, 4, 2, 4, 2)
CHIPS = ("zl", "y", "x", "zh")
DEAD = -(2.0**100)
ROWS = 64
META = 8
PARTS = 2


def packed_tiles(first, second):
    low = lax.broadcasted_iota(jnp.int32, (first.shape[0], HD), 1) < ROWS
    out = []
    for k in range(first.shape[1] // HD):
        a = first[:, k * HD : (k + 1) * HD]
        b = second[:, k * HD : (k + 1) * HD]
        crossed = pltpu.roll(jnp.where(low, b, a), ROWS, 1)
        out.append(jnp.where(low, a, crossed))
        out.append(jnp.where(low, crossed, b))
    return out


def partial_kernel(
    step, info, lengths, qa_ref, qb_ref, k0_ref, k1_ref, v0_ref, v1_ref, *rest
):
    oa_ref, ob_ref = rest[-2:]
    length = k0_ref.shape[1]
    leads, heads = qa_ref.shape[:2]
    width = 2 * leads * ROWS
    user = (info[1] + (KH - step)) % (lengths.shape[0] // 2)
    limit0 = lengths[info[0] + user] - info[2]
    limit1 = lengths[info[0] + user] - info[3]
    limits = (limit0, limit1)
    rows_dims = (((1,), (1,)), ((), ()))
    first_dims = (((0,), (0,)), ((), ()))

    def columns(j):
        if isinstance(j, int):
            return slice(j * HD, (j + 1) * HD)
        return pl.ds(pl.multiple_of(j * HD, HD), HD)

    def scores(j):
        cols = columns(j)
        q = jnp.concatenate(
            [
                qa_ref[:, j].reshape(width // 2, HD),
                qb_ref[:, j].reshape(width // 2, HD),
            ]
        )
        return [
            lax.dot_general(k[0, :, cols], q, rows_dims, preferred_element_type=jnp.float32)
            for k in (k0_ref, k1_ref)
        ]

    def weights(s, masked):
        s = [part * SCALE2 for part in s]
        if masked:
            at = lax.broadcasted_iota(jnp.int32, (length, width), 0)
            s = [jnp.where(at < limit, part, DEAD) for limit, part in zip(limits, s)]
        peak = jnp.maximum(*[jnp.max(part, axis=0, keepdims=True) for part in s])
        peak = peak.astype(jnp.bfloat16).astype(jnp.float32)
        w = [jnp.exp2(part - peak) for part in s]
        total = sum(jnp.sum(part, axis=0, keepdims=True) for part in w)
        return [part.astype(jnp.bfloat16) for part in w], total, peak

    def store(j, w, total, peak):
        cols = columns(j)
        numer = sum(
            lax.dot_general(
                v[0, :, cols], part, first_dims, preferred_element_type=jnp.float32
            )
            for v, part in zip((v0_ref, v1_ref), w)
        )
        numer = numer * (1.0 / total)
        high = total.astype(jnp.bfloat16).astype(jnp.float32)
        low = total - high
        top = lax.broadcasted_iota(jnp.int32, (META, width), 0) == 0
        tiles = packed_tiles(numer[:HALF], numer[HALF:])
        notes = packed_tiles(jnp.where(top, peak, low), jnp.where(top, high, low))
        for d in range(2 * leads):
            o_ref = oa_ref if d < leads else ob_ref
            o_ref[d % leads, j, :ROWS, :] = tiles[d].astype(jnp.bfloat16)
            o_ref[d % leads, j, ROWS:, :] = notes[d].astype(jnp.bfloat16)

    live = (limit0 >= length) & (limit1 >= length)

    @pl.when(live)
    def _():
        s = scores(0)
        for j in range(heads):
            ahead = scores(j + 1) if j + 1 < heads else None
            store(j, *weights(s, False))
            s = ahead

    dead = (limit0 <= 0) & (limit1 <= 0)

    @pl.when(dead)
    def _():
        shape = (heads, META, HD)
        side = lax.broadcasted_iota(jnp.int32, shape, 2) < ROWS
        first = lax.broadcasted_iota(jnp.int32, shape, 1) == 0
        note = jnp.where(first, jnp.where(side, DEAD, 1.0), 0.0).astype(jnp.bfloat16)
        for d in range(2 * leads):
            o_ref = oa_ref if d < leads else ob_ref
            o_ref[d % leads, :, :ROWS, :] = jnp.zeros((heads, ROWS, HD), jnp.bfloat16)
            o_ref[d % leads, :, ROWS:, :] = note

    @pl.when(jnp.logical_not(live | dead))
    def _():
        @pl.loop(0, heads)
        def _(j):
            store(j, *weights(scores(j), True))


def partials(step, info, lengths, qa, qb, k0, k1, v0, v1, parts=(0, PARTS), into=()):
    lead, heads = qa.shape[:2]
    length = k0.shape[1]
    share = heads // PARTS
    cache = (1, length, share * HD)
    begin, steps = parts
    half = lengths.shape[0] // 2

    def mine(p, info, lengths):
        return (info[0] + (info[1] + (KH - step)) % half, 0, begin + p)

    def other(p, info, lengths):
        return ((info[1] + (KH - step)) % half, 0, begin + p)

    def heads_at(p, info, lengths):
        return (0, begin + p, 0, 0)

    out = jax.ShapeDtypeStruct((lead, heads, ROWS + META, HD), jnp.bfloat16)
    asked = pl.BlockSpec((lead, share, ROWS, HD), heads_at)
    block = pl.BlockSpec((lead, share, ROWS + META, HD), heads_at)
    return pl.pallas_call(
        functools.partial(partial_kernel, step),
        grid_spec=pltpu.PrefetchScalarGridSpec(
            num_scalar_prefetch=2,
            grid=(steps,),
            in_specs=[
                asked,
                asked,
                pl.BlockSpec(cache, mine),
                pl.BlockSpec(cache, other),
                pl.BlockSpec(cache, mine),
                pl.BlockSpec(cache, other),
            ]
            + [pl.BlockSpec(memory_space=pl.ANY)] * len(into),
            out_specs=[block, block],
        ),
        out_shape=[out, out],
        input_output_aliases={8 + i: i for i in range(len(into))},
        compiler_params=pltpu.CompilerParams(
            dimension_semantics=("arbitrary",),
            vmem_limit_bytes=60 << 20,
        ),
        cost_estimate=pl.CostEstimate(
            flops=16 * share * steps * lead * ROWS * HD * length,
            bytes_accessed=8 * length * share * steps * HD,
            transcendentals=4 * share * steps * lead * ROWS * length,
        ),
    )(info, lengths, qa, qb, k0, k1, v0, v1, *into)


def stats_of(notes, low):
    line = notes[:1]
    turned = pltpu.roll(line, ROWS, 1)
    return jnp.where(low, line, turned), jnp.where(low, turned, line) + notes[1:2]


def merge_kernel(*refs):
    o_ref, w_ref = refs[-2:]
    low = lax.broadcasted_iota(jnp.int32, (8, HD), 1) < ROWS
    first = lax.broadcasted_iota(jnp.int32, (8, META, HD), 1) == 0

    def join(parts):
        def note(i, _):
            at = pl.ds(pl.multiple_of(i * 8, 8), 8)
            peaks, masses = [], []
            for r in parts:
                notes = r[at, ROWS:, :].astype(jnp.float32)
                line = notes[:, 0, :]
                turned = pltpu.roll(line, ROWS, 1)
                peaks.append(jnp.where(low, line, turned))
                masses.append(jnp.where(low, turned, line) + notes[:, 1, :])
            peak = functools.reduce(jnp.maximum, peaks)
            weights = [m * jnp.exp2(p - peak) for p, m in zip(peaks, masses)]
            total = functools.reduce(jnp.add, weights)
            inverse = 1.0 / total
            for n, w in enumerate(weights):
                w_ref[n, at, :] = w * inverse
            high = total.astype(jnp.bfloat16).astype(jnp.float32)
            line = jnp.where(low, peak, high)
            rest = total - high
            o_ref[at, ROWS:, :] = jnp.where(first, line[:, None], rest[:, None]).astype(
                jnp.bfloat16
            )
            return 0

        def add(t, _):
            acc = None
            for n, r in enumerate(parts):
                term = r[t, :ROWS, :].astype(jnp.float32) * w_ref[n, pl.ds(t, 1), :]
                acc = term if acc is None else acc + term
            o_ref[t, :ROWS, :] = acc.astype(jnp.bfloat16)
            return 0

        count = parts[0].shape[0]
        lax.fori_loop(0, count // 8, note, 0, unroll=2)
        lax.fori_loop(0, count, add, 0, unroll=4)

    per = (len(refs) - 2) // 2
    pl.when(pl.program_id(0) == 0)(lambda: join(refs[:per]))
    pl.when(pl.program_id(0) == 1)(lambda: join(refs[per : 2 * per]))


def merged(left, right):
    count, rows, _ = left[0].shape
    vmem = pl.BlockSpec(memory_space=pltpu.VMEM)
    return pl.pallas_call(
        merge_kernel,
        grid=(2,),
        in_specs=[vmem] * (len(left) + len(right)),
        out_specs=pl.BlockSpec((count, rows, HD), lambda i: (i, 0, 0)),
        scratch_shapes=[pltpu.VMEM((len(left), count, HD), jnp.float32)],
        out_shape=jax.ShapeDtypeStruct((2 * count, rows, HD), jnp.bfloat16),
        compiler_params=pltpu.CompilerParams(dimension_semantics=("arbitrary",), vmem_limit_bytes=52 << 20),
        cost_estimate=pl.CostEstimate(
            flops=16 * left[0].size, bytes_accessed=20 * left[0].size, transcendentals=0
        ),
    )(*left, *right)


def combine_kernel(holders, x_ref, own_ref, value_ref, o_ref, w_ref):
    users = value_ref.shape[0]
    low = lax.broadcasted_iota(jnp.int32, (1, HD), 1) < ROWS
    for u in range(users):
        own = own_ref[u]
        senders = [i for i, w in enumerate(holders) if w == u]
        pairs = [stats_of(x_ref[i, ROWS:, :].astype(jnp.float32), low) for i in senders]
        peak = own
        for top, _ in pairs:
            peak = jnp.maximum(peak, top)
        fresh = jnp.exp2(own - peak)
        total = fresh
        for i, (top, mass) in zip(senders, pairs):
            weight = mass * jnp.exp2(top - peak)
            w_ref[i : i + 1, :] = weight
            total = total + weight
        inverse = 1.0 / total
        acc = value_ref[u] * fresh
        for i in senders:
            acc = acc + x_ref[i, :ROWS, :].astype(jnp.float32) * w_ref[i : i + 1, :]
        turned = (acc * inverse).T
        o_ref[u] = jnp.concatenate([turned[:ROWS], turned[ROWS:]], axis=1).astype(
            jnp.bfloat16
        )


def combined(holders, x, own, value):
    users = value.shape[0]
    return pl.pallas_call(
        functools.partial(combine_kernel, holders),
        out_shape=jax.ShapeDtypeStruct((users, ROWS, HD), jnp.bfloat16),
        scratch_shapes=[pltpu.VMEM((x.shape[0], HD), jnp.float32)],
        compiler_params=pltpu.CompilerParams(vmem_limit_bytes=24 << 20),
        cost_estimate=pl.CostEstimate(
            flops=2 * x.size, bytes_accessed=2 * x.size, transcendentals=0
        ),
    )(x, own, value)


def moved(array, axis, step):
    count = SIZES[FINE.index(axis)]
    return lax.ppermute(array, axis, [(i, (i + step) % count) for i in range(count)])


def body(queries, key_cache, value_cache, key_table, value_table, lengths, token_ids):
    users, beams, _ = queries.shape
    half = users // 2
    length = key_cache.shape[1]
    x, y, zl, zh, c = (lax.axis_index(n) for n in ("x", "y", "zl", "zh", "c"))
    row = (zl * SIZES[1] + y) * 2 + c
    col = x * SIZES[4] + zh
    swap = functools.partial(lax.ppermute, axis_name="c", perm=[(0, 1), (1, 0)])

    def halves(array):
        return (
            lax.dynamic_slice_in_dim(array, c * half, half, 0),
            lax.dynamic_slice_in_dim(array, (1 - c) * half, half, 0),
        )

    q = queries.reshape(users, beams, GROUP, HD).transpose(0, 2, 1, 3)
    q_mine, q_give = halves(q)
    t_mine, t_give = halves(token_ids)
    q_give, t_give, key_source = lax.optimization_barrier((q_give, t_give, key_cache))
    q_chip = jnp.concatenate([q_mine, swap(q_give)], axis=2).reshape(half, ROWS, HD)
    tokens = jnp.concatenate([t_mine, swap(t_give)], axis=1)

    holders = [
        (a + b + 2 * h + l) % half
        for l in range(SIZES[0])
        for b in range(SIZES[1])
        for a in range(SIZES[3])
        for h in range(SIZES[4])
    ]
    chips = len(holders)
    held = (x + y + 2 * zh + zl) % half
    marks = np.asarray(holders).reshape(chips, 1, 1)
    operand = jnp.broadcast_to(q_chip[0], (chips, ROWS, HD))
    for w in range(1, half):
        operand = jnp.where(marks == w, q_chip[w], operand)
    operand, value_source = lax.optimization_barrier((operand, value_cache))
    got = lax.all_to_all(operand, CHIPS, 0, 0, tiled=True)
    got = got.reshape(chips // KH, KH, ROWS, HD)
    lead = chips // KH // 2
    got_a, got_b = got[:lead], got[lead:]

    k_other = swap(halves(key_source)[1])
    v_other = swap(halves(value_source)[1])
    got_a, got_b, k_other, v_other = lax.optimization_barrier(
        (got_a, got_b, k_other, v_other)
    )

    offset = (row * KH + col) * length
    other = ((row + 1 - 2 * c) * KH + col) * length

    info = jnp.stack([c * half, held, offset, other]).astype(jnp.int32)

    def computed(step, qa, qb, **kept):
        return partials(
            step, info, lengths, qa, qb, key_cache, k_other, value_cache, v_other, **kept
        )

    def flat(parts):
        return [p.reshape(-1, ROWS + META, HD) for p in parts]

    near = [(moved(got_a, "x", s), moved(got_b, "y", s)) for s in (1, -1)]
    begun = computed(0, got_a, got_b, parts=(0, PARTS // 2))
    near, begun, far_a, far_b = lax.optimization_barrier((near, begun, got_a, got_b))
    asked = {1: near[0], -1: near[1], 2: (moved(far_a, "x", 2), moved(far_b, "y", 2))}
    left, right = [], []
    for step, (qa, qb) in asked.items():
        parts = computed(step, qa, qb)
        one, two = flat(parts)
        left.append(moved(one, "x", -step))
        right.append(moved(two, "y", -step))
    begun, _ = lax.optimization_barrier((begun, parts))
    one, two = flat(
        computed(0, got_a, got_b, parts=(PARTS // 2, PARTS - PARTS // 2), into=begun)
    )
    left.append(one)
    right.append(two)
    arrived = lax.all_to_all(merged(left, right), CHIPS, 0, 0, tiled=True)

    codes = jnp.arange(key_table.shape[0], dtype=jnp.int32)
    onehot = (tokens[..., None] == codes).astype(jnp.bfloat16)
    keys = lax.dynamic_slice_in_dim(key_table, col * HD, HD, 1)
    values = lax.dynamic_slice_in_dim(value_table, col * HD, HD, 1)
    own_keys = jnp.einsum("uwv,vc->uwc", onehot, keys, preferred_element_type=jnp.float32)
    own_values = jnp.einsum("uwv,vc->uwc", onehot, values, preferred_element_type=jnp.float32)
    q_rows = q_chip.reshape(half, GROUP, 2 * beams, HD).astype(jnp.float32)
    own = jnp.sum(q_rows * own_keys[:, None], axis=-1) * SCALE2
    own = jnp.tile(own.reshape(half, 1, ROWS), (1, 1, 2))
    own_values = own_values.reshape(half, 2 * beams, 2, HALF).transpose(0, 3, 2, 1)
    own_values = jnp.broadcast_to(
        own_values[:, :, :, None], (half, HALF, 2, GROUP, 2 * beams)
    ).reshape(half, HALF, HD)

    result = combined(holders, arrived, own, own_values)
    result = result.reshape(half, GROUP, 2 * beams, HD)
    kept = result[:, :, :beams]
    received = swap(result[:, :, beams:])
    whole = jnp.where(
        c == 0, jnp.concatenate([kept, received]), jnp.concatenate([received, kept])
    )
    return whole.transpose(0, 2, 1, 3).reshape(users, beams, GROUP * HD)


def solution(mesh):
    fine = Mesh(np.asarray(mesh.devices).reshape(SIZES), FINE)
    row, col = ("zl", "y", "c"), ("x", "zh")
    return jax.shard_map(
        body,
        mesh=fine,
        in_specs=(
            P(None, row, col),
            P(None, row + col, None),
            P(None, row + col, None),
            P(),
            P(),
            P(),
            P(None, row),
        ),
        out_specs=P(None, row, col),
        check_vma=False,
    )
```

```python
import functools

import jax
import jax.numpy as jnp
import numpy as np
from jax import lax
from jax.experimental import pallas as pl
from jax.experimental.pallas import tpu as pltpu
from jax.sharding import Mesh
from jax.sharding import PartitionSpec as P

KH = 8
GROUP = 4
HD = 128
HALF = HD // 2
SCALE2 = HD**-0.5 * 1.4426950408889634
FINE = ("zl", "y", "c", "x", "zh")
SIZES = (2, 4, 2, 4, 2)
CHIPS = ("zl", "y", "x", "zh")
DEAD = -(2.0**100)
ROWS = 64
META = 8
PARTS = 2


def packed_tiles(first, second):
    low = lax.broadcasted_iota(jnp.int32, (first.shape[0], HD), 1) < ROWS
    out = []
    for k in range(first.shape[1] // HD):
        a = first[:, k * HD : (k + 1) * HD]
        b = second[:, k * HD : (k + 1) * HD]
        crossed = pltpu.roll(jnp.where(low, b, a), ROWS, 1)
        out.append(jnp.where(low, a, crossed))
        out.append(jnp.where(low, crossed, b))
    return out


def partial_kernel(step, asks, results, info, lengths, *refs):
    q_refs = refs[:asks]
    k0_ref, k1_ref, v0_ref, v1_ref = refs[asks : asks + 4]
    length = k0_ref.shape[1]
    heads = q_refs[0].shape[1]
    leads = sum(r.shape[0] for r in q_refs)
    o_refs = refs[len(refs) - results :]
    each = leads // len(o_refs)
    width = leads * ROWS
    user = (info[1] + (KH - step)) % (lengths.shape[0] // 2)
    limit0 = lengths[info[0] + user] - info[2]
    limit1 = lengths[info[0] + user] - info[3]
    limits = (limit0, limit1)
    rows_dims = (((1,), (1,)), ((), ()))
    first_dims = (((0,), (0,)), ((), ()))

    def columns(j):
        if isinstance(j, int):
            return slice(j * HD, (j + 1) * HD)
        return pl.ds(pl.multiple_of(j * HD, HD), HD)

    def scores(j):
        cols = columns(j)
        q = [r[:, j].reshape(r.shape[0] * ROWS, HD) for r in q_refs]
        q = jnp.concatenate(q) if len(q) > 1 else q[0]
        return [
            lax.dot_general(k[0, :, cols], q, rows_dims, preferred_element_type=jnp.float32)
            for k in (k0_ref, k1_ref)
        ]

    def weights(s, masked):
        s = [part * SCALE2 for part in s]
        if masked:
            at = lax.broadcasted_iota(jnp.int32, (length, width), 0)
            s = [jnp.where(at < limit, part, DEAD) for limit, part in zip(limits, s)]
        peak = jnp.maximum(*[jnp.max(part, axis=0, keepdims=True) for part in s])
        peak = peak.astype(jnp.bfloat16).astype(jnp.float32)
        w = [jnp.exp2(part - peak) for part in s]
        total = sum(jnp.sum(part, axis=0, keepdims=True) for part in w)
        return [part.astype(jnp.bfloat16) for part in w], total, peak

    def store(j, w, total, peak):
        cols = columns(j)
        numer = sum(
            lax.dot_general(
                v[0, :, cols], part, first_dims, preferred_element_type=jnp.float32
            )
            for v, part in zip((v0_ref, v1_ref), w)
        )
        numer = numer * (1.0 / total)
        high = total.astype(jnp.bfloat16).astype(jnp.float32)
        low = total - high
        top = lax.broadcasted_iota(jnp.int32, (META, width), 0) == 0
        tiles = packed_tiles(numer[:HALF], numer[HALF:])
        notes = packed_tiles(jnp.where(top, peak, low), jnp.where(top, high, low))
        for d in range(leads):
            o_refs[d // each][d % each, j, :ROWS, :] = tiles[d].astype(jnp.bfloat16)
            o_refs[d // each][d % each, j, ROWS:, :] = notes[d].astype(jnp.bfloat16)

    live = (limit0 >= length) & (limit1 >= length)

    @pl.when(live)
    def _():
        s = scores(0)
        for j in range(heads):
            ahead = scores(j + 1) if j + 1 < heads else None
            store(j, *weights(s, False))
            s = ahead

    dead = (limit0 <= 0) & (limit1 <= 0)

    @pl.when(dead)
    def _():
        shape = (heads, META, HD)
        side = lax.broadcasted_iota(jnp.int32, shape, 2) < ROWS
        first = lax.broadcasted_iota(jnp.int32, shape, 1) == 0
        note = jnp.where(first, jnp.where(side, DEAD, 1.0), 0.0).astype(jnp.bfloat16)
        for d in range(leads):
            empty = jnp.zeros((heads, ROWS, HD), jnp.bfloat16)
            o_refs[d // each][d % each, :, :ROWS, :] = empty
            o_refs[d // each][d % each, :, ROWS:, :] = note

    @pl.when(jnp.logical_not(live | dead))
    def _():
        @pl.loop(0, heads)
        def _(j):
            store(j, *weights(scores(j), True))


def partials(step, info, lengths, asked, caches, results=1, parts=(0, PARTS), into=()):
    heads = asked[0].shape[1]
    lead = sum(q.shape[0] for q in asked)
    length = caches[0].shape[1]
    share = heads // PARTS
    begin, steps = parts
    half = lengths.shape[0] // 2

    def mine(p, info, lengths):
        return (info[0] + (info[1] + (KH - step)) % half, 0, begin + p)

    def other(p, info, lengths):
        return ((info[1] + (KH - step)) % half, 0, begin + p)

    def heads_at(p, info, lengths):
        return (0, begin + p, 0, 0)

    cache = (1, length, share * HD)
    each = lead // results
    out = jax.ShapeDtypeStruct((each, heads, ROWS + META, HD), jnp.bfloat16)
    return pl.pallas_call(
        functools.partial(partial_kernel, step, len(asked), results),
        grid_spec=pltpu.PrefetchScalarGridSpec(
            num_scalar_prefetch=2,
            grid=(steps,),
            in_specs=[pl.BlockSpec((q.shape[0], share, ROWS, HD), heads_at) for q in asked]
            + [pl.BlockSpec(cache, mine), pl.BlockSpec(cache, other)] * 2
            + [pl.BlockSpec(memory_space=pl.ANY)] * len(into),
            out_specs=[pl.BlockSpec((each, share, ROWS + META, HD), heads_at)] * results,
        ),
        out_shape=[out] * results,
        input_output_aliases={6 + len(asked) + i: i for i in range(len(into))},
        compiler_params=pltpu.CompilerParams(
            dimension_semantics=("arbitrary",),
            vmem_limit_bytes=60 << 20,
        ),
        cost_estimate=pl.CostEstimate(
            flops=8 * share * steps * lead * ROWS * HD * length,
            bytes_accessed=8 * length * share * steps * HD,
            transcendentals=2 * share * steps * lead * ROWS * length,
        ),
    )(info, lengths, *asked, *caches, *into)


def stats_of(notes, low):
    line = notes[:1]
    turned = pltpu.roll(line, ROWS, 1)
    return jnp.where(low, line, turned), jnp.where(low, turned, line) + notes[1:2]


def merge_kernel(cuts, *refs):
    o_ref, w_ref = refs[-2:]
    count = o_ref.shape[0]
    low = lax.broadcasted_iota(jnp.int32, (8, HD), 1) < ROWS
    first = lax.broadcasted_iota(jnp.int32, (8, META, HD), 1) == 0

    def join(parts):
        def note(i, _):
            at = pl.ds(pl.multiple_of(i * 8, 8), 8)
            peaks, masses = [], []
            for r, base in parts:
                notes = r[pl.ds(pl.multiple_of(base + i * 8, 8), 8), ROWS:, :].astype(jnp.float32)
                line = notes[:, 0, :]
                turned = pltpu.roll(line, ROWS, 1)
                peaks.append(jnp.where(low, line, turned))
                masses.append(jnp.where(low, turned, line) + notes[:, 1, :])
            peak = functools.reduce(jnp.maximum, peaks)
            weights = [m * jnp.exp2(p - peak) for p, m in zip(peaks, masses)]
            total = functools.reduce(jnp.add, weights)
            inverse = 1.0 / total
            for n, w in enumerate(weights):
                w_ref[n, at, :] = w * inverse
            high = total.astype(jnp.bfloat16).astype(jnp.float32)
            line = jnp.where(low, peak, high)
            rest = total - high
            o_ref[at, ROWS:, :] = jnp.where(first, line[:, None], rest[:, None]).astype(
                jnp.bfloat16
            )
            return 0

        def add(t, _):
            acc = None
            for n, (r, base) in enumerate(parts):
                term = r[base + t, :ROWS, :].astype(jnp.float32) * w_ref[n, pl.ds(t, 1), :]
                acc = term if acc is None else acc + term
            o_ref[t, :ROWS, :] = acc.astype(jnp.bfloat16)
            return 0

        lax.fori_loop(0, count // 8, note, 0, unroll=2)
        lax.fori_loop(0, count, add, 0, unroll=4)

    for h in range(2):
        parts, at = [], 0
        for cut in cuts:
            parts.append((refs[at], h * count) if cut == 1 else (refs[at + h], 0))
            at += cut
        pl.when(pl.program_id(0) == h)(functools.partial(join, parts))


def merged(parts):
    cuts = [len(p) for p in parts]
    arrays = [array for p in parts for array in p]
    rows = ROWS + META
    total = sum(array.shape[0] for array in parts[0])
    vmem = pl.BlockSpec(memory_space=pltpu.VMEM)
    return pl.pallas_call(
        functools.partial(merge_kernel, cuts),
        grid=(2,),
        in_specs=[vmem] * len(arrays),
        out_specs=pl.BlockSpec((total // 2, rows, HD), lambda i: (i, 0, 0)),
        scratch_shapes=[pltpu.VMEM((len(parts), total // 2, HD), jnp.float32)],
        out_shape=jax.ShapeDtypeStruct((total, rows, HD), jnp.bfloat16),
        compiler_params=pltpu.CompilerParams(
            dimension_semantics=("arbitrary",), vmem_limit_bytes=52 << 20
        ),
        cost_estimate=pl.CostEstimate(
            flops=8 * total * rows * HD,
            bytes_accessed=10 * total * rows * HD,
            transcendentals=0,
        ),
    )(*arrays)


def combine_kernel(holders, x_ref, own_ref, value_ref, o_ref, w_ref):
    users = value_ref.shape[0]
    low = lax.broadcasted_iota(jnp.int32, (1, HD), 1) < ROWS
    for u in range(users):
        own = own_ref[u]
        senders = [i for i, w in enumerate(holders) if w == u]
        pairs = [stats_of(x_ref[i, ROWS:, :].astype(jnp.float32), low) for i in senders]
        peak = own
        for top, _ in pairs:
            peak = jnp.maximum(peak, top)
        fresh = jnp.exp2(own - peak)
        total = fresh
        for i, (top, mass) in zip(senders, pairs):
            weight = mass * jnp.exp2(top - peak)
            w_ref[i : i + 1, :] = weight
            total = total + weight
        inverse = 1.0 / total
        acc = value_ref[u] * fresh
        for i in senders:
            acc = acc + x_ref[i, :ROWS, :].astype(jnp.float32) * w_ref[i : i + 1, :]
        turned = (acc * inverse).T
        o_ref[u] = jnp.concatenate([turned[:ROWS], turned[ROWS:]], axis=1).astype(
            jnp.bfloat16
        )


def combined(holders, x, own, value):
    users = value.shape[0]
    return pl.pallas_call(
        functools.partial(combine_kernel, holders),
        out_shape=jax.ShapeDtypeStruct((users, ROWS, HD), jnp.bfloat16),
        scratch_shapes=[pltpu.VMEM((x.shape[0], HD), jnp.float32)],
        compiler_params=pltpu.CompilerParams(vmem_limit_bytes=24 << 20),
        cost_estimate=pl.CostEstimate(
            flops=2 * x.size, bytes_accessed=2 * x.size, transcendentals=0
        ),
    )(x, own, value)


def moved(array, axis, step):
    if axis == "z":
        at = [(z % 2) * 2 + z // 2 for z in range(4)]
        pairs = [(at[z], at[(z + step) % 4]) for z in range(4)]
        return lax.ppermute(array, ("zl", "zh"), pairs)
    count = SIZES[FINE.index(axis)]
    return lax.ppermute(array, axis, [(i, (i + step) % count) for i in range(count)])


def body(queries, key_cache, value_cache, key_table, value_table, lengths, token_ids):
    users, beams, _ = queries.shape
    half = users // 2
    length = key_cache.shape[1]
    x, y, zl, zh, c = (lax.axis_index(n) for n in ("x", "y", "zl", "zh", "c"))
    row = (zl * SIZES[1] + y) * 2 + c
    col = x * SIZES[4] + zh
    swap = functools.partial(lax.ppermute, axis_name="c", perm=[(0, 1), (1, 0)])

    def halves(array):
        return (
            lax.dynamic_slice_in_dim(array, c * half, half, 0),
            lax.dynamic_slice_in_dim(array, (1 - c) * half, half, 0),
        )

    q = queries.reshape(users, beams, GROUP, HD).transpose(0, 2, 1, 3)
    q_mine, q_give = halves(q)
    t_mine, t_give = halves(token_ids)
    q_give, t_give, key_source = lax.optimization_barrier((q_give, t_give, key_cache))
    q_chip = jnp.concatenate([q_mine, swap(q_give)], axis=2).reshape(half, ROWS, HD)
    tokens = jnp.concatenate([t_mine, swap(t_give)], axis=1)

    holders = [
        (a + b + 2 * h + l) % half
        for l in range(SIZES[0])
        for b in range(SIZES[1])
        for a in range(SIZES[3])
        for h in range(SIZES[4])
    ]
    chips = len(holders)
    held = (x + y + 2 * zh + zl) % half
    marks = np.asarray(holders).reshape(chips, 1, 1)
    operand = jnp.broadcast_to(q_chip[0], (chips, ROWS, HD))
    for w in range(1, half):
        operand = jnp.where(marks == w, q_chip[w], operand)
    operand, value_source = lax.optimization_barrier((operand, value_cache))
    got = lax.all_to_all(operand, CHIPS, 0, 0, tiled=True)
    got = got.reshape(chips // KH, KH, ROWS, HD)

    k_other = swap(halves(key_source)[1])
    v_other = swap(halves(value_source)[1])
    got, k_other, v_other = lax.optimization_barrier((got, k_other, v_other))

    offset = (row * KH + col) * length
    other = ((row + 1 - 2 * c) * KH + col) * length

    info = jnp.stack([c * half, held, offset, other]).astype(jnp.int32)

    caches = (key_cache, k_other, value_cache, v_other)
    lead = got.shape[0] // 2
    computed = functools.partial(partials, info=info, lengths=lengths, caches=caches)

    def flat(parts):
        return [p.reshape(-1, ROWS + META, HD) for p in parts]

    ask1 = [moved(got[:lead], "x", 1), moved(got[lead:], "y", 1)]
    ask3 = [moved(got, "z", -1)]
    begun = computed(0, asked=[got], parts=(0, PARTS // 2))
    ask1, begun, far = lax.optimization_barrier((ask1, begun, got))
    ask2 = [moved(far, "z", 2)]
    (sum1,) = flat(computed(1, asked=ask1))
    back = [[moved(sum1, "x", -1)]]
    ask3, sum1 = lax.optimization_barrier((ask3, sum1))
    (sum3,) = flat(computed(-1, asked=ask3))
    back.append([moved(sum3, "y", 1)])
    ask2, sum3 = lax.optimization_barrier((ask2, sum3))
    near, far = flat(computed(2, asked=ask2, results=2))
    back.append([moved(near, "x", -2), moved(far, "z", -2)])
    begun, _ = lax.optimization_barrier((begun, near))
    back.append(
        flat(computed(0, asked=[got], parts=(PARTS // 2, PARTS - PARTS // 2), into=begun))
    )
    arrived = lax.all_to_all(merged(back), CHIPS, 0, 0, tiled=True)

    codes = jnp.arange(key_table.shape[0], dtype=jnp.int32)
    onehot = (tokens[..., None] == codes).astype(jnp.bfloat16)
    keys = lax.dynamic_slice_in_dim(key_table, col * HD, HD, 1)
    values = lax.dynamic_slice_in_dim(value_table, col * HD, HD, 1)
    own_keys = jnp.einsum("uwv,vc->uwc", onehot, keys, preferred_element_type=jnp.float32)
    own_values = jnp.einsum("uwv,vc->uwc", onehot, values, preferred_element_type=jnp.float32)
    q_rows = q_chip.reshape(half, GROUP, 2 * beams, HD).astype(jnp.float32)
    own = jnp.sum(q_rows * own_keys[:, None], axis=-1) * SCALE2
    own = jnp.tile(own.reshape(half, 1, ROWS), (1, 1, 2))
    own_values = own_values.reshape(half, 2 * beams, 2, HALF).transpose(0, 3, 2, 1)
    own_values = jnp.broadcast_to(
        own_values[:, :, :, None], (half, HALF, 2, GROUP, 2 * beams)
    ).reshape(half, HALF, HD)

    result = combined(holders, arrived, own, own_values)
    result = result.reshape(half, GROUP, 2 * beams, HD)
    kept = result[:, :, :beams]
    received = swap(result[:, :, beams:])
    whole = jnp.where(
        c == 0, jnp.concatenate([kept, received]), jnp.concatenate([received, kept])
    )
    return whole.transpose(0, 2, 1, 3).reshape(users, beams, GROUP * HD)


def solution(mesh):
    fine = Mesh(np.asarray(mesh.devices).reshape(SIZES), FINE)
    row, col = ("zl", "y", "c"), ("x", "zh")
    return jax.shard_map(
        body,
        mesh=fine,
        in_specs=(
            P(None, row, col),
            P(None, row + col, None),
            P(None, row + col, None),
            P(),
            P(),
            P(),
            P(None, row),
        ),
        out_specs=P(None, row, col),
        check_vma=False,
    )
```

```python
import functools

import jax
import jax.numpy as jnp
import numpy as np
from jax import lax
from jax.experimental import pallas as pl
from jax.experimental.pallas import tpu as pltpu
from jax.sharding import Mesh
from jax.sharding import PartitionSpec as P

KH = 8
GROUP = 4
HD = 128
HALF = HD // 2
SCALE2 = HD**-0.5 * 1.4426950408889634
FINE = ("zl", "y", "c", "x", "zh")
SIZES = (2, 4, 2, 4, 2)
CHIPS = ("zl", "y", "x", "zh")
DEAD = -(2.0**100)
ROWS = 64
META = 8
PARTS = 2


def packed_tiles(first, second):
    low = lax.broadcasted_iota(jnp.int32, (first.shape[0], HD), 1) < ROWS
    out = []
    for k in range(first.shape[1] // HD):
        a = first[:, k * HD : (k + 1) * HD]
        b = second[:, k * HD : (k + 1) * HD]
        crossed = pltpu.roll(jnp.where(low, b, a), ROWS, 1)
        out.append(jnp.where(low, a, crossed))
        out.append(jnp.where(low, crossed, b))
    return out


def partial_kernel(step, asks, results, info, lengths, *refs):
    q_refs = refs[:asks]
    k0_ref, k1_ref, v0_ref, v1_ref = refs[asks : asks + 4]
    length = k0_ref.shape[1]
    heads = q_refs[0].shape[1]
    leads = sum(r.shape[0] for r in q_refs)
    o_refs = refs[len(refs) - results :]
    each = leads // len(o_refs)
    width = leads * ROWS
    user = (info[1] + (KH - step)) % (lengths.shape[0] // 2)
    limit0 = lengths[info[0] + user] - info[2]
    limit1 = lengths[info[0] + user] - info[3]
    limits = (limit0, limit1)
    rows_dims = (((1,), (1,)), ((), ()))
    first_dims = (((0,), (0,)), ((), ()))

    def columns(j):
        if isinstance(j, int):
            return slice(j * HD, (j + 1) * HD)
        return pl.ds(pl.multiple_of(j * HD, HD), HD)

    def scores(j):
        cols = columns(j)
        q = [r[:, j].reshape(r.shape[0] * ROWS, HD) for r in q_refs]
        q = jnp.concatenate(q) if len(q) > 1 else q[0]
        return [
            lax.dot_general(k[0, :, cols], q, rows_dims, preferred_element_type=jnp.float32)
            for k in (k0_ref, k1_ref)
        ]

    def weights(s, masked):
        s = [part * SCALE2 for part in s]
        if masked:
            at = lax.broadcasted_iota(jnp.int32, (length, width), 0)
            s = [jnp.where(at < limit, part, DEAD) for limit, part in zip(limits, s)]
        peak = jnp.maximum(*[jnp.max(part, axis=0, keepdims=True) for part in s])
        peak = peak.astype(jnp.bfloat16).astype(jnp.float32)
        w = [jnp.exp2(part - peak) for part in s]
        total = sum(jnp.sum(part, axis=0, keepdims=True) for part in w)
        return [part.astype(jnp.bfloat16) for part in w], total, peak

    def store(j, w, total, peak):
        cols = columns(j)
        numer = sum(
            lax.dot_general(
                v[0, :, cols], part, first_dims, preferred_element_type=jnp.float32
            )
            for v, part in zip((v0_ref, v1_ref), w)
        )
        numer = numer * (1.0 / total)
        high = total.astype(jnp.bfloat16).astype(jnp.float32)
        low = total - high
        top = lax.broadcasted_iota(jnp.int32, (META, width), 0) == 0
        tiles = packed_tiles(numer[:HALF], numer[HALF:])
        notes = packed_tiles(jnp.where(top, peak, low), jnp.where(top, high, low))
        for d in range(leads):
            o_refs[d // each][d % each, j, :ROWS, :] = tiles[d].astype(jnp.bfloat16)
            o_refs[d // each][d % each, j, ROWS:, :] = notes[d].astype(jnp.bfloat16)

    live = (limit0 >= length) & (limit1 >= length)

    @pl.when(live)
    def _():
        s = scores(0)
        for j in range(heads):
            ahead = scores(j + 1) if j + 1 < heads else None
            store(j, *weights(s, False))
            s = ahead

    dead = (limit0 <= 0) & (limit1 <= 0)

    @pl.when(dead)
    def _():
        shape = (heads, META, HD)
        side = lax.broadcasted_iota(jnp.int32, shape, 2) < ROWS
        first = lax.broadcasted_iota(jnp.int32, shape, 1) == 0
        note = jnp.where(first, jnp.where(side, DEAD, 1.0), 0.0).astype(jnp.bfloat16)
        for d in range(leads):
            empty = jnp.zeros((heads, ROWS, HD), jnp.bfloat16)
            o_refs[d // each][d % each, :, :ROWS, :] = empty
            o_refs[d // each][d % each, :, ROWS:, :] = note

    @pl.when(jnp.logical_not(live | dead))
    def _():
        @pl.loop(0, heads)
        def _(j):
            store(j, *weights(scores(j), True))


def partials(step, info, lengths, asked, caches, results=1, parts=(0, PARTS), into=()):
    heads = asked[0].shape[1]
    lead = sum(q.shape[0] for q in asked)
    length = caches[0].shape[1]
    share = heads // PARTS
    begin, steps = parts
    half = lengths.shape[0] // 2

    def mine(p, info, lengths):
        return (info[0] + (info[1] + (KH - step)) % half, 0, begin + p)

    def other(p, info, lengths):
        return ((info[1] + (KH - step)) % half, 0, begin + p)

    def heads_at(p, info, lengths):
        return (0, begin + p, 0, 0)

    cache = (1, length, share * HD)
    each = lead // results
    out = jax.ShapeDtypeStruct((each, heads, ROWS + META, HD), jnp.bfloat16)
    return pl.pallas_call(
        functools.partial(partial_kernel, step, len(asked), results),
        grid_spec=pltpu.PrefetchScalarGridSpec(
            num_scalar_prefetch=2,
            grid=(steps,),
            in_specs=[pl.BlockSpec((q.shape[0], share, ROWS, HD), heads_at) for q in asked]
            + [pl.BlockSpec(cache, mine), pl.BlockSpec(cache, other)] * 2
            + [pl.BlockSpec(memory_space=pl.ANY)] * len(into),
            out_specs=[pl.BlockSpec((each, share, ROWS + META, HD), heads_at)] * results,
        ),
        out_shape=[out] * results,
        input_output_aliases={6 + len(asked) + i: i for i in range(len(into))},
        compiler_params=pltpu.CompilerParams(
            dimension_semantics=("arbitrary",),
            vmem_limit_bytes=60 << 20,
        ),
        cost_estimate=pl.CostEstimate(
            flops=8 * share * steps * lead * ROWS * HD * length,
            bytes_accessed=8 * length * share * steps * HD,
            transcendentals=2 * share * steps * lead * ROWS * length,
        ),
    )(info, lengths, *asked, *caches, *into)


def stats_of(notes, low):
    line = notes[:1]
    turned = pltpu.roll(line, ROWS, 1)
    return jnp.where(low, line, turned), jnp.where(low, turned, line) + notes[1:2]


def merge_kernel(cuts, *refs):
    o_ref, w_ref = refs[-2:]
    count = o_ref.shape[0]
    low = lax.broadcasted_iota(jnp.int32, (8, HD), 1) < ROWS
    first = lax.broadcasted_iota(jnp.int32, (8, META, HD), 1) == 0

    def join(parts):
        def note(i, _):
            at = pl.ds(pl.multiple_of(i * 8, 8), 8)
            peaks, masses = [], []
            for r, base in parts:
                notes = r[pl.ds(pl.multiple_of(base + i * 8, 8), 8), ROWS:, :].astype(jnp.float32)
                line = notes[:, 0, :]
                turned = pltpu.roll(line, ROWS, 1)
                peaks.append(jnp.where(low, line, turned))
                masses.append(jnp.where(low, turned, line) + notes[:, 1, :])
            peak = functools.reduce(jnp.maximum, peaks)
            weights = [m * jnp.exp2(p - peak) for p, m in zip(peaks, masses)]
            total = functools.reduce(jnp.add, weights)
            inverse = 1.0 / total
            for n, w in enumerate(weights):
                w_ref[n, at, :] = w * inverse
            high = total.astype(jnp.bfloat16).astype(jnp.float32)
            line = jnp.where(low, peak, high)
            rest = total - high
            o_ref[at, ROWS:, :] = jnp.where(first, line[:, None], rest[:, None]).astype(
                jnp.bfloat16
            )
            return 0

        def add(t, _):
            acc = None
            for n, (r, base) in enumerate(parts):
                term = r[base + t, :ROWS, :].astype(jnp.float32) * w_ref[n, pl.ds(t, 1), :]
                acc = term if acc is None else acc + term
            o_ref[t, :ROWS, :] = acc.astype(jnp.bfloat16)
            return 0

        lax.fori_loop(0, count // 8, note, 0, unroll=2)
        lax.fori_loop(0, count, add, 0, unroll=4)

    for h in range(2):
        parts, at = [], 0
        for cut in cuts:
            parts.append((refs[at], h * count) if cut == 1 else (refs[at + h], 0))
            at += cut
        pl.when(pl.program_id(0) == h)(functools.partial(join, parts))


def merged(parts):
    cuts = [len(p) for p in parts]
    arrays = [array for p in parts for array in p]
    rows = ROWS + META
    total = sum(array.shape[0] for array in parts[0])
    vmem = pl.BlockSpec(memory_space=pltpu.VMEM)
    return pl.pallas_call(
        functools.partial(merge_kernel, cuts),
        grid=(2,),
        in_specs=[vmem] * len(arrays),
        out_specs=pl.BlockSpec((total // 2, rows, HD), lambda i: (i, 0, 0)),
        scratch_shapes=[pltpu.VMEM((len(parts), total // 2, HD), jnp.float32)],
        out_shape=jax.ShapeDtypeStruct((total, rows, HD), jnp.bfloat16),
        compiler_params=pltpu.CompilerParams(
            dimension_semantics=("arbitrary",), vmem_limit_bytes=52 << 20
        ),
        cost_estimate=pl.CostEstimate(
            flops=8 * total * rows * HD,
            bytes_accessed=10 * total * rows * HD,
            transcendentals=0,
        ),
    )(*arrays)


def combine_kernel(holders, x_ref, own_ref, value_ref, o_ref, w_ref):
    users = value_ref.shape[0]
    low = lax.broadcasted_iota(jnp.int32, (1, HD), 1) < ROWS
    for u in range(users):
        own = own_ref[u]
        senders = [i for i, w in enumerate(holders) if w == u]
        pairs = [stats_of(x_ref[i, ROWS:, :].astype(jnp.float32), low) for i in senders]
        peak = own
        for top, _ in pairs:
            peak = jnp.maximum(peak, top)
        fresh = jnp.exp2(own - peak)
        total = fresh
        for i, (top, mass) in zip(senders, pairs):
            weight = mass * jnp.exp2(top - peak)
            w_ref[i : i + 1, :] = weight
            total = total + weight
        inverse = 1.0 / total
        acc = value_ref[u] * fresh
        for i in senders:
            acc = acc + x_ref[i, :ROWS, :].astype(jnp.float32) * w_ref[i : i + 1, :]
        turned = (acc * inverse).T
        o_ref[u] = jnp.concatenate([turned[:ROWS], turned[ROWS:]], axis=1).astype(
            jnp.bfloat16
        )


def combined(holders, x, own, value):
    users = value.shape[0]
    return pl.pallas_call(
        functools.partial(combine_kernel, holders),
        out_shape=jax.ShapeDtypeStruct((users, ROWS, HD), jnp.bfloat16),
        scratch_shapes=[pltpu.VMEM((x.shape[0], HD), jnp.float32)],
        compiler_params=pltpu.CompilerParams(vmem_limit_bytes=24 << 20),
        cost_estimate=pl.CostEstimate(
            flops=2 * x.size, bytes_accessed=2 * x.size, transcendentals=0
        ),
    )(x, own, value)


def moved(array, axis, step):
    if axis == "z":
        at = [(z % 2) * 2 + z // 2 for z in range(4)]
        pairs = [(at[z], at[(z + step) % 4]) for z in range(4)]
        return lax.ppermute(array, ("zl", "zh"), pairs)
    count = SIZES[FINE.index(axis)]
    return lax.ppermute(array, axis, [(i, (i + step) % count) for i in range(count)])


def body(queries, key_cache, value_cache, key_table, value_table, lengths, token_ids):
    users, beams, _ = queries.shape
    half = users // 2
    length = key_cache.shape[1]
    x, y, zl, zh, c = (lax.axis_index(n) for n in ("x", "y", "zl", "zh", "c"))
    row = (zl * SIZES[1] + y) * 2 + c
    col = x * SIZES[4] + zh
    swap = functools.partial(lax.ppermute, axis_name="c", perm=[(0, 1), (1, 0)])

    def halves(array):
        return (
            lax.dynamic_slice_in_dim(array, c * half, half, 0),
            lax.dynamic_slice_in_dim(array, (1 - c) * half, half, 0),
        )

    q = queries.reshape(users, beams, GROUP, HD).transpose(0, 2, 1, 3)
    q_mine, q_give = halves(q)
    t_mine, t_give = halves(token_ids)
    q_give, t_give, key_source = lax.optimization_barrier((q_give, t_give, key_cache))
    q_chip = jnp.concatenate([q_mine, swap(q_give)], axis=2).reshape(half, ROWS, HD)
    tokens = jnp.concatenate([t_mine, swap(t_give)], axis=1)

    holders = [
        (a + b + 2 * h + l) % half
        for l in range(SIZES[0])
        for b in range(SIZES[1])
        for a in range(SIZES[3])
        for h in range(SIZES[4])
    ]
    chips = len(holders)
    held = (x + y + 2 * zh + zl) % half
    marks = np.asarray(holders).reshape(chips, 1, 1)
    operand = jnp.broadcast_to(q_chip[0], (chips, ROWS, HD))
    for w in range(1, half):
        operand = jnp.where(marks == w, q_chip[w], operand)
    operand, value_source = lax.optimization_barrier((operand, value_cache))
    got = lax.all_to_all(operand, CHIPS, 0, 0, tiled=True)
    got = got.reshape(chips // KH, KH, ROWS, HD)

    k_other = swap(halves(key_source)[1])
    v_other = swap(halves(value_source)[1])
    got, k_other, v_other = lax.optimization_barrier((got, k_other, v_other))

    offset = (row * KH + col) * length
    other = ((row + 1 - 2 * c) * KH + col) * length

    info = jnp.stack([c * half, held, offset, other]).astype(jnp.int32)

    caches = (key_cache, k_other, value_cache, v_other)
    lead = got.shape[0] // 2
    computed = functools.partial(partials, info=info, lengths=lengths, caches=caches)

    def flat(parts):
        return [p.reshape(-1, ROWS + META, HD) for p in parts]

    ask1 = [moved(got[:lead], "x", 1), moved(got[lead:], "y", 1)]
    ask3 = [moved(got[:lead], "x", -1), moved(got[lead:], "y", -1)]
    ask2 = [moved(got, "z", 2)]
    begun = computed(0, asked=[got], parts=(0, PARTS // 2))
    ask1, ask3, begun = lax.optimization_barrier((ask1, ask3, begun))
    (sum1,) = flat(computed(1, asked=ask1))
    back = [[moved(sum1, "x", -1)]]
    ask3, sum1 = lax.optimization_barrier((ask3, sum1))
    (sum3,) = flat(computed(-1, asked=ask3))
    back.append([moved(sum3, "y", 1)])
    ask2, sum3 = lax.optimization_barrier((ask2, sum3))
    near, far = flat(computed(2, asked=ask2, results=2))
    back.append([moved(near, "x", -2), moved(far, "z", -2)])
    begun, _ = lax.optimization_barrier((begun, near))
    back.append(
        flat(computed(0, asked=[got], parts=(PARTS // 2, PARTS - PARTS // 2), into=begun))
    )
    arrived = lax.all_to_all(merged(back), CHIPS, 0, 0, tiled=True)

    codes = jnp.arange(key_table.shape[0], dtype=jnp.int32)
    onehot = (tokens[..., None] == codes).astype(jnp.bfloat16)
    keys = lax.dynamic_slice_in_dim(key_table, col * HD, HD, 1)
    values = lax.dynamic_slice_in_dim(value_table, col * HD, HD, 1)
    own_keys = jnp.einsum("uwv,vc->uwc", onehot, keys, preferred_element_type=jnp.float32)
    own_values = jnp.einsum("uwv,vc->uwc", onehot, values, preferred_element_type=jnp.float32)
    q_rows = q_chip.reshape(half, GROUP, 2 * beams, HD).astype(jnp.float32)
    own = jnp.sum(q_rows * own_keys[:, None], axis=-1) * SCALE2
    own = jnp.tile(own.reshape(half, 1, ROWS), (1, 1, 2))
    own_values = own_values.reshape(half, 2 * beams, 2, HALF).transpose(0, 3, 2, 1)
    own_values = jnp.broadcast_to(
        own_values[:, :, :, None], (half, HALF, 2, GROUP, 2 * beams)
    ).reshape(half, HALF, HD)

    result = combined(holders, arrived, own, own_values)
    result = result.reshape(half, GROUP, 2 * beams, HD)
    kept = result[:, :, :beams]
    received = swap(result[:, :, beams:])
    whole = jnp.where(
        c == 0, jnp.concatenate([kept, received]), jnp.concatenate([received, kept])
    )
    return whole.transpose(0, 2, 1, 3).reshape(users, beams, GROUP * HD)


def solution(mesh):
    fine = Mesh(np.asarray(mesh.devices).reshape(SIZES), FINE)
    row, col = ("zl", "y", "c"), ("x", "zh")
    return jax.shard_map(
        body,
        mesh=fine,
        in_specs=(
            P(None, row, col),
            P(None, row + col, None),
            P(None, row + col, None),
            P(),
            P(),
            P(),
            P(None, row),
        ),
        out_specs=P(None, row, col),
        check_vma=False,
    )
```

```python
import functools

import jax
import jax.numpy as jnp
import numpy as np
from jax import lax
from jax.experimental import pallas as pl
from jax.experimental.pallas import tpu as pltpu
from jax.sharding import Mesh
from jax.sharding import PartitionSpec as P

KH = 8
GROUP = 4
HD = 128
HALF = HD // 2
SCALE2 = HD**-0.5 * 1.4426950408889634
FINE = ("zl", "y", "c", "x", "zh")
SIZES = (2, 4, 2, 4, 2)
CHIPS = ("zl", "y", "x", "zh")
DEAD = -(2.0**100)
ROWS = 64
META = 8
PARTS = 2


def packed_tiles(first, second):
    low = lax.broadcasted_iota(jnp.int32, (first.shape[0], HD), 1) < ROWS
    out = []
    for k in range(first.shape[1] // HD):
        a = first[:, k * HD : (k + 1) * HD]
        b = second[:, k * HD : (k + 1) * HD]
        crossed = pltpu.roll(jnp.where(low, b, a), ROWS, 1)
        out.append(jnp.where(low, a, crossed))
        out.append(jnp.where(low, crossed, b))
    return out


def partial_kernel(step, asks, results, info, lengths, *refs):
    q_refs = refs[:asks]
    k0_ref, k1_ref, v0_ref, v1_ref = refs[asks : asks + 4]
    length = k0_ref.shape[1]
    heads = q_refs[0].shape[1]
    leads = sum(r.shape[0] for r in q_refs)
    o_refs = refs[len(refs) - results :]
    each = leads // len(o_refs)
    width = leads * ROWS
    user = (info[1] + (KH - step)) % (lengths.shape[0] // 2)
    limit0 = lengths[info[0] + user] - info[2]
    limit1 = lengths[info[0] + user] - info[3]
    limits = (limit0, limit1)
    rows_dims = (((1,), (1,)), ((), ()))
    first_dims = (((0,), (0,)), ((), ()))

    def columns(j):
        if isinstance(j, int):
            return slice(j * HD, (j + 1) * HD)
        return pl.ds(pl.multiple_of(j * HD, HD), HD)

    def scores(j):
        cols = columns(j)
        q = [r[:, j].reshape(r.shape[0] * ROWS, HD) for r in q_refs]
        q = jnp.concatenate(q) if len(q) > 1 else q[0]
        return [
            lax.dot_general(k[0, :, cols], q, rows_dims, preferred_element_type=jnp.float32)
            for k in (k0_ref, k1_ref)
        ]

    def weights(s, masked):
        s = [part * SCALE2 for part in s]
        if masked:
            at = lax.broadcasted_iota(jnp.int32, (length, width), 0)
            s = [jnp.where(at < limit, part, DEAD) for limit, part in zip(limits, s)]
        peak = jnp.maximum(*[jnp.max(part, axis=0, keepdims=True) for part in s])
        peak = peak.astype(jnp.bfloat16).astype(jnp.float32)
        w = [jnp.exp2(part - peak) for part in s]
        total = sum(jnp.sum(part, axis=0, keepdims=True) for part in w)
        return [part.astype(jnp.bfloat16) for part in w], total, peak

    def store(j, w, total, peak):
        cols = columns(j)
        numer = sum(
            lax.dot_general(
                v[0, :, cols], part, first_dims, preferred_element_type=jnp.float32
            )
            for v, part in zip((v0_ref, v1_ref), w)
        )
        numer = numer * (1.0 / total)
        high = total.astype(jnp.bfloat16).astype(jnp.float32)
        low = total - high
        top = lax.broadcasted_iota(jnp.int32, (META, width), 0) == 0
        tiles = packed_tiles(numer[:HALF], numer[HALF:])
        notes = packed_tiles(jnp.where(top, peak, low), jnp.where(top, high, low))
        for d in range(leads):
            o_refs[d // each][d % each, j, :ROWS, :] = tiles[d].astype(jnp.bfloat16)
            o_refs[d // each][d % each, j, ROWS:, :] = notes[d].astype(jnp.bfloat16)

    live = (limit0 >= length) & (limit1 >= length)

    @pl.when(live)
    def _():
        s = scores(0)
        for j in range(heads):
            ahead = scores(j + 1) if j + 1 < heads else None
            store(j, *weights(s, False))
            s = ahead

    dead = (limit0 <= 0) & (limit1 <= 0)

    @pl.when(dead)
    def _():
        shape = (heads, META, HD)
        side = lax.broadcasted_iota(jnp.int32, shape, 2) < ROWS
        first = lax.broadcasted_iota(jnp.int32, shape, 1) == 0
        note = jnp.where(first, jnp.where(side, DEAD, 1.0), 0.0).astype(jnp.bfloat16)
        for d in range(leads):
            empty = jnp.zeros((heads, ROWS, HD), jnp.bfloat16)
            o_refs[d // each][d % each, :, :ROWS, :] = empty
            o_refs[d // each][d % each, :, ROWS:, :] = note

    @pl.when(jnp.logical_not(live | dead))
    def _():
        @pl.loop(0, heads)
        def _(j):
            store(j, *weights(scores(j), True))


def partials(step, info, lengths, asked, caches, results=1, parts=(0, PARTS), into=()):
    heads = asked[0].shape[1]
    lead = sum(q.shape[0] for q in asked)
    length = caches[0].shape[1]
    share = heads // PARTS
    begin, steps = parts
    half = lengths.shape[0] // 2

    def mine(p, info, lengths):
        return (info[0] + (info[1] + (KH - step)) % half, 0, begin + p)

    def other(p, info, lengths):
        return ((info[1] + (KH - step)) % half, 0, begin + p)

    def heads_at(p, info, lengths):
        return (0, begin + p, 0, 0)

    cache = (1, length, share * HD)
    each = lead // results
    out = jax.ShapeDtypeStruct((each, heads, ROWS + META, HD), jnp.bfloat16)
    return pl.pallas_call(
        functools.partial(partial_kernel, step, len(asked), results),
        grid_spec=pltpu.PrefetchScalarGridSpec(
            num_scalar_prefetch=2,
            grid=(steps,),
            in_specs=[pl.BlockSpec((q.shape[0], share, ROWS, HD), heads_at) for q in asked]
            + [pl.BlockSpec(cache, mine), pl.BlockSpec(cache, other)] * 2
            + [pl.BlockSpec(memory_space=pl.ANY)] * len(into),
            out_specs=[pl.BlockSpec((each, share, ROWS + META, HD), heads_at)] * results,
        ),
        out_shape=[out] * results,
        input_output_aliases={6 + len(asked) + i: i for i in range(len(into))},
        compiler_params=pltpu.CompilerParams(
            dimension_semantics=("arbitrary",),
            vmem_limit_bytes=60 << 20,
        ),
        cost_estimate=pl.CostEstimate(
            flops=8 * share * steps * lead * ROWS * HD * length,
            bytes_accessed=8 * length * share * steps * HD,
            transcendentals=2 * share * steps * lead * ROWS * length,
        ),
    )(info, lengths, *asked, *caches, *into)


def stats_of(notes, low):
    line = notes[:1]
    turned = pltpu.roll(line, ROWS, 1)
    return jnp.where(low, line, turned), jnp.where(low, turned, line) + notes[1:2]


def merge_kernel(cuts, *refs):
    o_ref, w_ref = refs[-2:]
    count = o_ref.shape[0]
    low = lax.broadcasted_iota(jnp.int32, (8, HD), 1) < ROWS
    first = lax.broadcasted_iota(jnp.int32, (8, META, HD), 1) == 0

    def join(parts):
        def note(i, _):
            at = pl.ds(pl.multiple_of(i * 8, 8), 8)
            peaks, masses = [], []
            for r, base in parts:
                notes = r[pl.ds(pl.multiple_of(base + i * 8, 8), 8), ROWS:, :].astype(jnp.float32)
                line = notes[:, 0, :]
                turned = pltpu.roll(line, ROWS, 1)
                peaks.append(jnp.where(low, line, turned))
                masses.append(jnp.where(low, turned, line) + notes[:, 1, :])
            peak = functools.reduce(jnp.maximum, peaks)
            weights = [m * jnp.exp2(p - peak) for p, m in zip(peaks, masses)]
            total = functools.reduce(jnp.add, weights)
            inverse = 1.0 / total
            for n, w in enumerate(weights):
                w_ref[n, at, :] = w * inverse
            high = total.astype(jnp.bfloat16).astype(jnp.float32)
            line = jnp.where(low, peak, high)
            rest = total - high
            o_ref[at, ROWS:, :] = jnp.where(first, line[:, None], rest[:, None]).astype(
                jnp.bfloat16
            )
            return 0

        def add(t, _):
            acc = None
            for n, (r, base) in enumerate(parts):
                term = r[base + t, :ROWS, :].astype(jnp.float32) * w_ref[n, pl.ds(t, 1), :]
                acc = term if acc is None else acc + term
            o_ref[t, :ROWS, :] = acc.astype(jnp.bfloat16)
            return 0

        lax.fori_loop(0, count // 8, note, 0, unroll=2)
        lax.fori_loop(0, count, add, 0, unroll=4)

    for h in range(2):
        parts, at = [], 0
        for cut in cuts:
            parts.append((refs[at], h * count) if cut == 1 else (refs[at + h], 0))
            at += cut
        pl.when(pl.program_id(0) == h)(functools.partial(join, parts))


def merged(parts):
    cuts = [len(p) for p in parts]
    arrays = [array for p in parts for array in p]
    rows = ROWS + META
    total = sum(array.shape[0] for array in parts[0])
    vmem = pl.BlockSpec(memory_space=pltpu.VMEM)
    return pl.pallas_call(
        functools.partial(merge_kernel, cuts),
        grid=(2,),
        in_specs=[vmem] * len(arrays),
        out_specs=pl.BlockSpec((total // 2, rows, HD), lambda i: (i, 0, 0)),
        scratch_shapes=[pltpu.VMEM((len(parts), total // 2, HD), jnp.float32)],
        out_shape=jax.ShapeDtypeStruct((total, rows, HD), jnp.bfloat16),
        compiler_params=pltpu.CompilerParams(
            dimension_semantics=("arbitrary",), vmem_limit_bytes=52 << 20
        ),
        cost_estimate=pl.CostEstimate(
            flops=8 * total * rows * HD,
            bytes_accessed=10 * total * rows * HD,
            transcendentals=0,
        ),
    )(*arrays)


def combine_kernel(holders, x_ref, own_ref, value_ref, o_ref, w_ref):
    users = value_ref.shape[0]
    low = lax.broadcasted_iota(jnp.int32, (1, HD), 1) < ROWS
    for u in range(users):
        own = own_ref[u]
        senders = [i for i, w in enumerate(holders) if w == u]
        pairs = [stats_of(x_ref[i, ROWS:, :].astype(jnp.float32), low) for i in senders]
        peak = own
        for top, _ in pairs:
            peak = jnp.maximum(peak, top)
        fresh = jnp.exp2(own - peak)
        total = fresh
        for i, (top, mass) in zip(senders, pairs):
            weight = mass * jnp.exp2(top - peak)
            w_ref[i : i + 1, :] = weight
            total = total + weight
        inverse = 1.0 / total
        acc = value_ref[u] * fresh
        for i in senders:
            acc = acc + x_ref[i, :ROWS, :].astype(jnp.float32) * w_ref[i : i + 1, :]
        turned = (acc * inverse).T
        o_ref[u] = jnp.concatenate([turned[:ROWS], turned[ROWS:]], axis=1).astype(
            jnp.bfloat16
        )


def combined(holders, x, own, value):
    users = value.shape[0]
    return pl.pallas_call(
        functools.partial(combine_kernel, holders),
        out_shape=jax.ShapeDtypeStruct((users, ROWS, HD), jnp.bfloat16),
        scratch_shapes=[pltpu.VMEM((x.shape[0], HD), jnp.float32)],
        compiler_params=pltpu.CompilerParams(vmem_limit_bytes=24 << 20),
        cost_estimate=pl.CostEstimate(
            flops=2 * x.size, bytes_accessed=2 * x.size, transcendentals=0
        ),
    )(x, own, value)


def moved(array, axis, step):
    if axis == "z":
        at = [(z % 2) * 2 + z // 2 for z in range(4)]
        pairs = [(at[z], at[(z + step) % 4]) for z in range(4)]
        return lax.ppermute(array, ("zl", "zh"), pairs)
    count = SIZES[FINE.index(axis)]
    return lax.ppermute(array, axis, [(i, (i + step) % count) for i in range(count)])


def body(queries, key_cache, value_cache, key_table, value_table, lengths, token_ids):
    users, beams, _ = queries.shape
    half = users // 2
    length = key_cache.shape[1]
    x, y, zl, zh, c = (lax.axis_index(n) for n in ("x", "y", "zl", "zh", "c"))
    row = (zl * SIZES[1] + y) * 2 + c
    col = x * SIZES[4] + zh
    swap = functools.partial(lax.ppermute, axis_name="c", perm=[(0, 1), (1, 0)])

    def halves(array):
        return (
            lax.dynamic_slice_in_dim(array, c * half, half, 0),
            lax.dynamic_slice_in_dim(array, (1 - c) * half, half, 0),
        )

    q = queries.reshape(users, beams, GROUP, HD).transpose(0, 2, 1, 3)
    q_mine, q_give = halves(q)
    t_mine, t_give = halves(token_ids)
    q_give, t_give, key_source = lax.optimization_barrier((q_give, t_give, key_cache))
    q_chip = jnp.concatenate([q_mine, swap(q_give)], axis=2).reshape(half, ROWS, HD)
    tokens = jnp.concatenate([t_mine, swap(t_give)], axis=1)

    holders = [
        (a + b + 2 * h + l) % half
        for l in range(SIZES[0])
        for b in range(SIZES[1])
        for a in range(SIZES[3])
        for h in range(SIZES[4])
    ]
    chips = len(holders)
    held = (x + y + 2 * zh + zl) % half
    marks = np.asarray(holders).reshape(chips, 1, 1)
    operand = jnp.broadcast_to(q_chip[0], (chips, ROWS, HD))
    for w in range(1, half):
        operand = jnp.where(marks == w, q_chip[w], operand)
    operand, value_source = lax.optimization_barrier((operand, value_cache))
    got = lax.all_to_all(operand, CHIPS, 0, 0, tiled=True)
    got = got.reshape(chips // KH, KH, ROWS, HD)

    k_other = swap(halves(key_source)[1])
    v_other = swap(halves(value_source)[1])
    got, k_other, v_other = lax.optimization_barrier((got, k_other, v_other))

    offset = (row * KH + col) * length
    other = ((row + 1 - 2 * c) * KH + col) * length

    info = jnp.stack([c * half, held, offset, other]).astype(jnp.int32)

    caches = (key_cache, k_other, value_cache, v_other)
    lead = got.shape[0] // 2
    computed = functools.partial(partials, info=info, lengths=lengths, caches=caches)

    def flat(parts):
        return [p.reshape(-1, ROWS + META, HD) for p in parts]

    ask1 = [moved(got[:lead], "x", 1), moved(got[lead:], "y", 1)]
    ask3 = [moved(got[:lead], "x", -1), moved(got[lead:], "y", -1)]
    ask2 = [moved(got, "z", 2)]
    begun = computed(0, asked=[got], parts=(0, PARTS // 2))
    ask1, ask3, begun = lax.optimization_barrier((ask1, ask3, begun))
    near, far = flat(computed(1, asked=ask1, results=2))
    back = [[moved(near, "x", -1), moved(far, "y", -1)]]
    ask3, _ = lax.optimization_barrier((ask3, near))
    near, far = flat(computed(-1, asked=ask3, results=2))
    back.append([moved(near, "x", 1), moved(far, "y", 1)])
    ask2, _ = lax.optimization_barrier((ask2, near))
    near, far = flat(computed(2, asked=ask2, results=2))
    back.append([moved(near, "x", -2), moved(far, "z", -2)])
    begun, _ = lax.optimization_barrier((begun, near))
    back.append(
        flat(computed(0, asked=[got], parts=(PARTS // 2, PARTS - PARTS // 2), into=begun))
    )
    arrived = lax.all_to_all(merged(back), CHIPS, 0, 0, tiled=True)

    codes = jnp.arange(key_table.shape[0], dtype=jnp.int32)
    onehot = (tokens[..., None] == codes).astype(jnp.bfloat16)
    keys = lax.dynamic_slice_in_dim(key_table, col * HD, HD, 1)
    values = lax.dynamic_slice_in_dim(value_table, col * HD, HD, 1)
    own_keys = jnp.einsum("uwv,vc->uwc", onehot, keys, preferred_element_type=jnp.float32)
    own_values = jnp.einsum("uwv,vc->uwc", onehot, values, preferred_element_type=jnp.float32)
    q_rows = q_chip.reshape(half, GROUP, 2 * beams, HD).astype(jnp.float32)
    own = jnp.sum(q_rows * own_keys[:, None], axis=-1) * SCALE2
    own = jnp.tile(own.reshape(half, 1, ROWS), (1, 1, 2))
    own_values = own_values.reshape(half, 2 * beams, 2, HALF).transpose(0, 3, 2, 1)
    own_values = jnp.broadcast_to(
        own_values[:, :, :, None], (half, HALF, 2, GROUP, 2 * beams)
    ).reshape(half, HALF, HD)

    result = combined(holders, arrived, own, own_values)
    result = result.reshape(half, GROUP, 2 * beams, HD)
    kept = result[:, :, :beams]
    received = swap(result[:, :, beams:])
    whole = jnp.where(
        c == 0, jnp.concatenate([kept, received]), jnp.concatenate([received, kept])
    )
    return whole.transpose(0, 2, 1, 3).reshape(users, beams, GROUP * HD)


def solution(mesh):
    fine = Mesh(np.asarray(mesh.devices).reshape(SIZES), FINE)
    row, col = ("zl", "y", "c"), ("x", "zh")
    return jax.shard_map(
        body,
        mesh=fine,
        in_specs=(
            P(None, row, col),
            P(None, row + col, None),
            P(None, row + col, None),
            P(),
            P(),
            P(),
            P(None, row),
        ),
        out_specs=P(None, row, col),
        check_vma=False,
    )
```

```python
import functools

import jax
import jax.numpy as jnp
import numpy as np
from jax import lax
from jax.experimental import pallas as pl
from jax.experimental.pallas import tpu as pltpu
from jax.sharding import Mesh
from jax.sharding import PartitionSpec as P

KH = 8
GROUP = 4
HD = 128
HALF = HD // 2
SCALE2 = HD**-0.5 * 1.4426950408889634
FINE = ("zl", "y", "c", "x", "zh")
SIZES = (2, 4, 2, 4, 2)
CHIPS = ("zl", "y", "x", "zh")
DEAD = -(2.0**100)
ROWS = 64
META = 8
PARTS = 2


def packed_tiles(first, second):
    low = lax.broadcasted_iota(jnp.int32, (first.shape[0], HD), 1) < ROWS
    out = []
    for k in range(first.shape[1] // HD):
        a = first[:, k * HD : (k + 1) * HD]
        b = second[:, k * HD : (k + 1) * HD]
        crossed = pltpu.roll(jnp.where(low, b, a), ROWS, 1)
        out.append(jnp.where(low, a, crossed))
        out.append(jnp.where(low, crossed, b))
    return out


def partial_kernel(step, asks, results, info, lengths, *refs):
    q_refs = refs[:asks]
    k0_ref, k1_ref, v0_ref, v1_ref = refs[asks : asks + 4]
    length = k0_ref.shape[1]
    heads = q_refs[0].shape[1]
    leads = sum(r.shape[0] for r in q_refs)
    o_refs = refs[len(refs) - results :]
    each = leads // len(o_refs)
    width = leads * ROWS
    user = (info[1] + (KH - step)) % (lengths.shape[0] // 2)
    limit0 = lengths[info[0] + user] - info[2]
    limit1 = lengths[info[0] + user] - info[3]
    limits = (limit0, limit1)
    rows_dims = (((1,), (1,)), ((), ()))
    first_dims = (((0,), (0,)), ((), ()))

    def columns(j):
        if isinstance(j, int):
            return slice(j * HD, (j + 1) * HD)
        return pl.ds(pl.multiple_of(j * HD, HD), HD)

    def scores(j):
        cols = columns(j)
        q = [r[:, j].reshape(r.shape[0] * ROWS, HD) for r in q_refs]
        q = jnp.concatenate(q) if len(q) > 1 else q[0]
        return [
            lax.dot_general(k[0, :, cols], q, rows_dims, preferred_element_type=jnp.float32)
            for k in (k0_ref, k1_ref)
        ]

    def weights(s, masked):
        s = [part * SCALE2 for part in s]
        if masked:
            at = lax.broadcasted_iota(jnp.int32, (length, width), 0)
            s = [jnp.where(at < limit, part, DEAD) for limit, part in zip(limits, s)]
        peak = jnp.maximum(*[jnp.max(part, axis=0, keepdims=True) for part in s])
        peak = peak.astype(jnp.bfloat16).astype(jnp.float32)
        w = [jnp.exp2(part - peak) for part in s]
        total = sum(jnp.sum(part, axis=0, keepdims=True) for part in w)
        return [part.astype(jnp.bfloat16) for part in w], total, peak

    def store(j, w, total, peak):
        cols = columns(j)
        numer = sum(
            lax.dot_general(
                v[0, :, cols], part, first_dims, preferred_element_type=jnp.float32
            )
            for v, part in zip((v0_ref, v1_ref), w)
        )
        numer = numer * (1.0 / total)
        high = total.astype(jnp.bfloat16).astype(jnp.float32)
        low = total - high
        top = lax.broadcasted_iota(jnp.int32, (META, width), 0) == 0
        tiles = packed_tiles(numer[:HALF], numer[HALF:])
        notes = packed_tiles(jnp.where(top, peak, low), jnp.where(top, high, low))
        for d in range(leads):
            o_refs[d // each][d % each, j, :ROWS, :] = tiles[d].astype(jnp.bfloat16)
            o_refs[d // each][d % each, j, ROWS:, :] = notes[d].astype(jnp.bfloat16)

    live = (limit0 >= length) & (limit1 >= length)

    @pl.when(live)
    def _():
        s = scores(0)
        for j in range(heads):
            ahead = scores(j + 1) if j + 1 < heads else None
            store(j, *weights(s, False))
            s = ahead

    dead = (limit0 <= 0) & (limit1 <= 0)

    @pl.when(dead)
    def _():
        shape = (heads, META, HD)
        side = lax.broadcasted_iota(jnp.int32, shape, 2) < ROWS
        first = lax.broadcasted_iota(jnp.int32, shape, 1) == 0
        note = jnp.where(first, jnp.where(side, DEAD, 1.0), 0.0).astype(jnp.bfloat16)
        for d in range(leads):
            empty = jnp.zeros((heads, ROWS, HD), jnp.bfloat16)
            o_refs[d // each][d % each, :, :ROWS, :] = empty
            o_refs[d // each][d % each, :, ROWS:, :] = note

    @pl.when(jnp.logical_not(live | dead))
    def _():
        @pl.loop(0, heads)
        def _(j):
            store(j, *weights(scores(j), True))


def partials(step, info, lengths, asked, caches, results=1, parts=(0, PARTS), into=()):
    heads = asked[0].shape[1]
    lead = sum(q.shape[0] for q in asked)
    length = caches[0].shape[1]
    share = heads // PARTS
    begin, steps = parts
    half = lengths.shape[0] // 2

    def mine(p, info, lengths):
        return (info[0] + (info[1] + (KH - step)) % half, 0, begin + p)

    def other(p, info, lengths):
        return ((info[1] + (KH - step)) % half, 0, begin + p)

    def heads_at(p, info, lengths):
        return (0, begin + p, 0, 0)

    cache = (1, length, share * HD)
    each = lead // results
    out = jax.ShapeDtypeStruct((each, heads, ROWS + META, HD), jnp.bfloat16)
    return pl.pallas_call(
        functools.partial(partial_kernel, step, len(asked), results),
        grid_spec=pltpu.PrefetchScalarGridSpec(
            num_scalar_prefetch=2,
            grid=(steps,),
            in_specs=[pl.BlockSpec((q.shape[0], share, ROWS, HD), heads_at) for q in asked]
            + [pl.BlockSpec(cache, mine), pl.BlockSpec(cache, other)] * 2
            + [pl.BlockSpec(memory_space=pl.ANY)] * len(into),
            out_specs=[pl.BlockSpec((each, share, ROWS + META, HD), heads_at)] * results,
        ),
        out_shape=[out] * results,
        input_output_aliases={6 + len(asked) + i: i for i in range(len(into))},
        compiler_params=pltpu.CompilerParams(
            dimension_semantics=("arbitrary",),
            vmem_limit_bytes=60 << 20,
        ),
        cost_estimate=pl.CostEstimate(
            flops=8 * share * steps * lead * ROWS * HD * length,
            bytes_accessed=8 * length * share * steps * HD,
            transcendentals=2 * share * steps * lead * ROWS * length,
        ),
    )(info, lengths, *asked, *caches, *into)


def stats_of(notes, low):
    line = notes[:1]
    turned = pltpu.roll(line, ROWS, 1)
    return jnp.where(low, line, turned), jnp.where(low, turned, line) + notes[1:2]


def merge_kernel(cuts, *refs):
    o_ref, w_ref = refs[-2:]
    count = o_ref.shape[0]
    low = lax.broadcasted_iota(jnp.int32, (8, HD), 1) < ROWS
    first = lax.broadcasted_iota(jnp.int32, (8, META, HD), 1) == 0

    def join(parts):
        def note(i, _):
            at = pl.ds(pl.multiple_of(i * 8, 8), 8)
            peaks, masses = [], []
            for r, base in parts:
                notes = r[pl.ds(pl.multiple_of(base + i * 8, 8), 8), ROWS:, :].astype(jnp.float32)
                line = notes[:, 0, :]
                turned = pltpu.roll(line, ROWS, 1)
                peaks.append(jnp.where(low, line, turned))
                masses.append(jnp.where(low, turned, line) + notes[:, 1, :])
            peak = functools.reduce(jnp.maximum, peaks)
            weights = [m * jnp.exp2(p - peak) for p, m in zip(peaks, masses)]
            total = functools.reduce(jnp.add, weights)
            inverse = 1.0 / total
            for n, w in enumerate(weights):
                w_ref[n, at, :] = w * inverse
            high = total.astype(jnp.bfloat16).astype(jnp.float32)
            line = jnp.where(low, peak, high)
            rest = total - high
            o_ref[at, ROWS:, :] = jnp.where(first, line[:, None], rest[:, None]).astype(
                jnp.bfloat16
            )
            return 0

        def add(t, _):
            acc = None
            for n, (r, base) in enumerate(parts):
                term = r[base + t, :ROWS, :].astype(jnp.float32) * w_ref[n, pl.ds(t, 1), :]
                acc = term if acc is None else acc + term
            o_ref[t, :ROWS, :] = acc.astype(jnp.bfloat16)
            return 0

        lax.fori_loop(0, count // 8, note, 0, unroll=2)
        lax.fori_loop(0, count, add, 0, unroll=4)

    for h in range(2):
        parts, at = [], 0
        for cut in cuts:
            parts.append((refs[at], h * count) if cut == 1 else (refs[at + h], 0))
            at += cut
        pl.when(pl.program_id(0) == h)(functools.partial(join, parts))


def merged(parts):
    cuts = [len(p) for p in parts]
    arrays = [array for p in parts for array in p]
    rows = ROWS + META
    total = sum(array.shape[0] for array in parts[0])
    vmem = pl.BlockSpec(memory_space=pltpu.VMEM)
    return pl.pallas_call(
        functools.partial(merge_kernel, cuts),
        grid=(2,),
        in_specs=[vmem] * len(arrays),
        out_specs=pl.BlockSpec((total // 2, rows, HD), lambda i: (i, 0, 0)),
        scratch_shapes=[pltpu.VMEM((len(parts), total // 2, HD), jnp.float32)],
        out_shape=jax.ShapeDtypeStruct((total, rows, HD), jnp.bfloat16),
        compiler_params=pltpu.CompilerParams(
            dimension_semantics=("arbitrary",), vmem_limit_bytes=52 << 20
        ),
        cost_estimate=pl.CostEstimate(
            flops=8 * total * rows * HD,
            bytes_accessed=10 * total * rows * HD,
            transcendentals=0,
        ),
    )(*arrays)


def combine_kernel(holders, x_ref, own_ref, value_ref, o_ref, w_ref):
    users = value_ref.shape[0]
    low = lax.broadcasted_iota(jnp.int32, (1, HD), 1) < ROWS
    for u in range(users):
        own = own_ref[u]
        senders = [i for i, w in enumerate(holders) if w == u]
        pairs = [stats_of(x_ref[i, ROWS:, :].astype(jnp.float32), low) for i in senders]
        peak = own
        for top, _ in pairs:
            peak = jnp.maximum(peak, top)
        fresh = jnp.exp2(own - peak)
        total = fresh
        for i, (top, mass) in zip(senders, pairs):
            weight = mass * jnp.exp2(top - peak)
            w_ref[i : i + 1, :] = weight
            total = total + weight
        inverse = 1.0 / total
        acc = value_ref[u] * fresh
        for i in senders:
            acc = acc + x_ref[i, :ROWS, :].astype(jnp.float32) * w_ref[i : i + 1, :]
        turned = (acc * inverse).T
        o_ref[u] = jnp.concatenate([turned[:ROWS], turned[ROWS:]], axis=1).astype(
            jnp.bfloat16
        )


def combined(holders, x, own, value):
    users = value.shape[0]
    return pl.pallas_call(
        functools.partial(combine_kernel, holders),
        out_shape=jax.ShapeDtypeStruct((users, ROWS, HD), jnp.bfloat16),
        scratch_shapes=[pltpu.VMEM((x.shape[0], HD), jnp.float32)],
        compiler_params=pltpu.CompilerParams(vmem_limit_bytes=24 << 20),
        cost_estimate=pl.CostEstimate(
            flops=2 * x.size, bytes_accessed=2 * x.size, transcendentals=0
        ),
    )(x, own, value)


def moved(array, axis, step):
    if axis == "z":
        at = [(z % 2) * 2 + z // 2 for z in range(4)]
        pairs = [(at[z], at[(z + step) % 4]) for z in range(4)]
        return lax.ppermute(array, ("zl", "zh"), pairs)
    count = SIZES[FINE.index(axis)]
    return lax.ppermute(array, axis, [(i, (i + step) % count) for i in range(count)])


def body(queries, key_cache, value_cache, key_table, value_table, lengths, token_ids):
    users, beams, _ = queries.shape
    half = users // 2
    length = key_cache.shape[1]
    x, y, zl, zh, c = (lax.axis_index(n) for n in ("x", "y", "zl", "zh", "c"))
    row = (zl * SIZES[1] + y) * 2 + c
    col = x * SIZES[4] + zh
    swap = functools.partial(lax.ppermute, axis_name="c", perm=[(0, 1), (1, 0)])

    def halves(array):
        return (
            lax.dynamic_slice_in_dim(array, c * half, half, 0),
            lax.dynamic_slice_in_dim(array, (1 - c) * half, half, 0),
        )

    q = queries.reshape(users, beams, GROUP, HD).transpose(0, 2, 1, 3)
    q_mine, q_give = halves(q)
    t_mine, t_give = halves(token_ids)
    q_give, t_give, key_source = lax.optimization_barrier((q_give, t_give, key_cache))
    q_chip = jnp.concatenate([q_mine, swap(q_give)], axis=2).reshape(half, ROWS, HD)
    tokens = jnp.concatenate([t_mine, swap(t_give)], axis=1)

    holders = [
        (a + b + 2 * h + l) % half
        for l in range(SIZES[0])
        for b in range(SIZES[1])
        for a in range(SIZES[3])
        for h in range(SIZES[4])
    ]
    chips = len(holders)
    held = (x + y + 2 * zh + zl) % half
    marks = np.asarray(holders).reshape(chips, 1, 1)
    operand = jnp.broadcast_to(q_chip[0], (chips, ROWS, HD))
    for w in range(1, half):
        operand = jnp.where(marks == w, q_chip[w], operand)
    operand, value_source = lax.optimization_barrier((operand, value_cache))
    got = lax.all_to_all(operand, CHIPS, 0, 0, tiled=True)
    got = got.reshape(chips // KH, KH, ROWS, HD)

    k_other = swap(halves(key_source)[1])
    v_other = swap(halves(value_source)[1])
    got, k_other, v_other = lax.optimization_barrier((got, k_other, v_other))

    offset = (row * KH + col) * length
    other = ((row + 1 - 2 * c) * KH + col) * length

    info = jnp.stack([c * half, held, offset, other]).astype(jnp.int32)

    caches = (key_cache, k_other, value_cache, v_other)
    lead = got.shape[0] // 2
    computed = functools.partial(partials, info=info, lengths=lengths, caches=caches)

    def flat(parts):
        return [p.reshape(-1, ROWS + META, HD) for p in parts]

    ask1 = [moved(got[:lead], "x", 1), moved(got[lead:], "y", 1)]
    ask3 = [moved(got[:lead], "x", -1), moved(got[lead:], "y", -1)]
    ask2 = [moved(got, "z", 2)]
    begun = computed(0, asked=[got], parts=(0, PARTS // 2))
    ask1, ask3, begun = lax.optimization_barrier((ask1, ask3, begun))
    near, far = flat(computed(1, asked=ask1, results=2))
    back = [[moved(near, "x", -1), moved(far, "y", -1)]]
    ask3, _ = lax.optimization_barrier((ask3, near))
    near, far = flat(computed(-1, asked=ask3, results=2))
    back.append([moved(near, "x", 1), moved(far, "y", 1)])
    ask2, _, back[0] = lax.optimization_barrier((ask2, near, back[0]))
    near, far = flat(computed(2, asked=ask2, results=2))
    back.append([moved(near, "x", -2), moved(far, "z", -2)])
    begun, _ = lax.optimization_barrier((begun, near))
    back.append(
        flat(computed(0, asked=[got], parts=(PARTS // 2, PARTS - PARTS // 2), into=begun))
    )
    arrived = lax.all_to_all(merged(back), CHIPS, 0, 0, tiled=True)

    codes = jnp.arange(key_table.shape[0], dtype=jnp.int32)
    onehot = (tokens[..., None] == codes).astype(jnp.bfloat16)
    keys = lax.dynamic_slice_in_dim(key_table, col * HD, HD, 1)
    values = lax.dynamic_slice_in_dim(value_table, col * HD, HD, 1)
    own_keys = jnp.einsum("uwv,vc->uwc", onehot, keys, preferred_element_type=jnp.float32)
    own_values = jnp.einsum("uwv,vc->uwc", onehot, values, preferred_element_type=jnp.float32)
    q_rows = q_chip.reshape(half, GROUP, 2 * beams, HD).astype(jnp.float32)
    own = jnp.sum(q_rows * own_keys[:, None], axis=-1) * SCALE2
    own = jnp.tile(own.reshape(half, 1, ROWS), (1, 1, 2))
    own_values = own_values.reshape(half, 2 * beams, 2, HALF).transpose(0, 3, 2, 1)
    own_values = jnp.broadcast_to(
        own_values[:, :, :, None], (half, HALF, 2, GROUP, 2 * beams)
    ).reshape(half, HALF, HD)

    result = combined(holders, arrived, own, own_values)
    result = result.reshape(half, GROUP, 2 * beams, HD)
    kept = result[:, :, :beams]
    received = swap(result[:, :, beams:])
    whole = jnp.where(
        c == 0, jnp.concatenate([kept, received]), jnp.concatenate([received, kept])
    )
    return whole.transpose(0, 2, 1, 3).reshape(users, beams, GROUP * HD)


def solution(mesh):
    fine = Mesh(np.asarray(mesh.devices).reshape(SIZES), FINE)
    row, col = ("zl", "y", "c"), ("x", "zh")
    return jax.shard_map(
        body,
        mesh=fine,
        in_specs=(
            P(None, row, col),
            P(None, row + col, None),
            P(None, row + col, None),
            P(),
            P(),
            P(),
            P(None, row),
        ),
        out_specs=P(None, row, col),
        check_vma=False,
    )
```

```python
import functools

import jax
import jax.numpy as jnp
import numpy as np
from jax import lax
from jax.experimental import pallas as pl
from jax.experimental.pallas import tpu as pltpu
from jax.sharding import Mesh
from jax.sharding import PartitionSpec as P

KH = 8
GROUP = 4
HD = 128
HALF = HD // 2
SCALE2 = HD**-0.5 * 1.4426950408889634
FINE = ("zl", "y", "c", "x", "zh")
SIZES = (2, 4, 2, 4, 2)
CHIPS = ("zl", "y", "x", "zh")
DEAD = -(2.0**100)
ROWS = 64
META = 8
PARTS = 2


def packed_tiles(first, second):
    low = lax.broadcasted_iota(jnp.int32, (first.shape[0], HD), 1) < ROWS
    out = []
    for k in range(first.shape[1] // HD):
        a = first[:, k * HD : (k + 1) * HD]
        b = second[:, k * HD : (k + 1) * HD]
        crossed = pltpu.roll(jnp.where(low, b, a), ROWS, 1)
        out.append(jnp.where(low, a, crossed))
        out.append(jnp.where(low, crossed, b))
    return out


def partial_kernel(step, asks, results, info, lengths, *refs):
    q_refs = refs[:asks]
    k0_ref, k1_ref, v0_ref, v1_ref = refs[asks : asks + 4]
    length = k0_ref.shape[1]
    heads = q_refs[0].shape[1]
    leads = sum(r.shape[0] for r in q_refs)
    o_refs = refs[len(refs) - results :]
    each = leads // len(o_refs)
    width = leads * ROWS
    user = (info[1] + (KH - step)) % (lengths.shape[0] // 2)
    limit0 = lengths[info[0] + user] - info[2]
    limit1 = lengths[info[0] + user] - info[3]
    limits = (limit0, limit1)
    rows_dims = (((1,), (1,)), ((), ()))
    first_dims = (((0,), (0,)), ((), ()))

    def columns(j):
        if isinstance(j, int):
            return slice(j * HD, (j + 1) * HD)
        return pl.ds(pl.multiple_of(j * HD, HD), HD)

    def scores(j):
        cols = columns(j)
        q = [r[:, j].reshape(r.shape[0] * ROWS, HD) for r in q_refs]
        q = jnp.concatenate(q) if len(q) > 1 else q[0]
        return [
            lax.dot_general(k[0, :, cols], q, rows_dims, preferred_element_type=jnp.float32)
            for k in (k0_ref, k1_ref)
        ]

    def weights(s, masked):
        s = [part * SCALE2 for part in s]
        if masked:
            at = lax.broadcasted_iota(jnp.int32, (length, width), 0)
            s = [jnp.where(at < limit, part, DEAD) for limit, part in zip(limits, s)]
        peak = jnp.maximum(*[jnp.max(part, axis=0, keepdims=True) for part in s])
        peak = peak.astype(jnp.bfloat16).astype(jnp.float32)
        w = [jnp.exp2(part - peak) for part in s]
        total = sum(jnp.sum(part, axis=0, keepdims=True) for part in w)
        return [part.astype(jnp.bfloat16) for part in w], total, peak

    def store(j, w, total, peak):
        cols = columns(j)
        numer = sum(
            lax.dot_general(
                v[0, :, cols], part, first_dims, preferred_element_type=jnp.float32
            )
            for v, part in zip((v0_ref, v1_ref), w)
        )
        numer = numer * (1.0 / total)
        high = total.astype(jnp.bfloat16).astype(jnp.float32)
        low = total - high
        top = lax.broadcasted_iota(jnp.int32, (META, width), 0) == 0
        tiles = packed_tiles(numer[:HALF], numer[HALF:])
        notes = packed_tiles(jnp.where(top, peak, low), jnp.where(top, high, low))
        for d in range(leads):
            o_refs[d // each][d % each, j, :ROWS, :] = tiles[d].astype(jnp.bfloat16)
            o_refs[d // each][d % each, j, ROWS:, :] = notes[d].astype(jnp.bfloat16)

    live = (limit0 >= length) & (limit1 >= length)

    @pl.when(live)
    def _():
        s = scores(0)
        for j in range(heads):
            ahead = scores(j + 1) if j + 1 < heads else None
            store(j, *weights(s, False))
            s = ahead

    dead = (limit0 <= 0) & (limit1 <= 0)

    @pl.when(dead)
    def _():
        shape = (heads, META, HD)
        side = lax.broadcasted_iota(jnp.int32, shape, 2) < ROWS
        first = lax.broadcasted_iota(jnp.int32, shape, 1) == 0
        note = jnp.where(first, jnp.where(side, DEAD, 1.0), 0.0).astype(jnp.bfloat16)
        for d in range(leads):
            empty = jnp.zeros((heads, ROWS, HD), jnp.bfloat16)
            o_refs[d // each][d % each, :, :ROWS, :] = empty
            o_refs[d // each][d % each, :, ROWS:, :] = note

    @pl.when(jnp.logical_not(live | dead))
    def _():
        @pl.loop(0, heads)
        def _(j):
            store(j, *weights(scores(j), True))


def partials(step, info, lengths, asked, caches, results=1, parts=(0, PARTS), into=()):
    heads = asked[0].shape[1]
    lead = sum(q.shape[0] for q in asked)
    length = caches[0].shape[1]
    share = heads // PARTS
    begin, steps = parts
    half = lengths.shape[0] // 2

    def mine(p, info, lengths):
        return (info[0] + (info[1] + (KH - step)) % half, 0, begin + p)

    def other(p, info, lengths):
        return ((info[1] + (KH - step)) % half, 0, begin + p)

    def heads_at(p, info, lengths):
        return (0, begin + p, 0, 0)

    cache = (1, length, share * HD)
    each = lead // results
    out = jax.ShapeDtypeStruct((each, heads, ROWS + META, HD), jnp.bfloat16)
    return pl.pallas_call(
        functools.partial(partial_kernel, step, len(asked), results),
        grid_spec=pltpu.PrefetchScalarGridSpec(
            num_scalar_prefetch=2,
            grid=(steps,),
            in_specs=[pl.BlockSpec((q.shape[0], share, ROWS, HD), heads_at) for q in asked]
            + [pl.BlockSpec(cache, mine), pl.BlockSpec(cache, other)] * 2
            + [pl.BlockSpec(memory_space=pl.ANY)] * len(into),
            out_specs=[pl.BlockSpec((each, share, ROWS + META, HD), heads_at)] * results,
        ),
        out_shape=[out] * results,
        input_output_aliases={6 + len(asked) + i: i for i in range(len(into))},
        compiler_params=pltpu.CompilerParams(
            dimension_semantics=("arbitrary",),
            vmem_limit_bytes=60 << 20,
        ),
        cost_estimate=pl.CostEstimate(
            flops=8 * share * steps * lead * ROWS * HD * length,
            bytes_accessed=8 * length * share * steps * HD,
            transcendentals=2 * share * steps * lead * ROWS * length,
        ),
    )(info, lengths, *asked, *caches, *into)


def stats_of(notes, low):
    line = notes[:1]
    turned = pltpu.roll(line, ROWS, 1)
    return jnp.where(low, line, turned), jnp.where(low, turned, line) + notes[1:2]


def merge_kernel(cuts, *refs):
    o_ref, w_ref = refs[-2:]
    count = o_ref.shape[0]
    low = lax.broadcasted_iota(jnp.int32, (8, HD), 1) < ROWS
    first = lax.broadcasted_iota(jnp.int32, (8, META, HD), 1) == 0

    def join(parts):
        def note(i, _):
            at = pl.ds(pl.multiple_of(i * 8, 8), 8)
            peaks, masses = [], []
            for r, base in parts:
                notes = r[pl.ds(pl.multiple_of(base + i * 8, 8), 8), ROWS:, :].astype(jnp.float32)
                line = notes[:, 0, :]
                turned = pltpu.roll(line, ROWS, 1)
                peaks.append(jnp.where(low, line, turned))
                masses.append(jnp.where(low, turned, line) + notes[:, 1, :])
            peak = functools.reduce(jnp.maximum, peaks)
            weights = [m * jnp.exp2(p - peak) for p, m in zip(peaks, masses)]
            total = functools.reduce(jnp.add, weights)
            inverse = 1.0 / total
            for n, w in enumerate(weights):
                w_ref[n, at, :] = w * inverse
            high = total.astype(jnp.bfloat16).astype(jnp.float32)
            line = jnp.where(low, peak, high)
            rest = total - high
            o_ref[at, ROWS:, :] = jnp.where(first, line[:, None], rest[:, None]).astype(
                jnp.bfloat16
            )
            return 0

        def add(t, _):
            acc = None
            for n, (r, base) in enumerate(parts):
                term = r[base + t, :ROWS, :].astype(jnp.float32) * w_ref[n, pl.ds(t, 1), :]
                acc = term if acc is None else acc + term
            o_ref[t, :ROWS, :] = acc.astype(jnp.bfloat16)
            return 0

        lax.fori_loop(0, count // 8, note, 0, unroll=4)
        lax.fori_loop(0, count, add, 0, unroll=8)

    for h in range(2):
        parts, at = [], 0
        for cut in cuts:
            parts.append((refs[at], h * count) if cut == 1 else (refs[at + h], 0))
            at += cut
        pl.when(pl.program_id(0) == h)(functools.partial(join, parts))


def merged(parts):
    cuts = [len(p) for p in parts]
    arrays = [array for p in parts for array in p]
    rows = ROWS + META
    total = sum(array.shape[0] for array in parts[0])
    vmem = pl.BlockSpec(memory_space=pltpu.VMEM)
    return pl.pallas_call(
        functools.partial(merge_kernel, cuts),
        grid=(2,),
        in_specs=[vmem] * len(arrays),
        out_specs=pl.BlockSpec((total // 2, rows, HD), lambda i: (i, 0, 0)),
        scratch_shapes=[pltpu.VMEM((len(parts), total // 2, HD), jnp.float32)],
        out_shape=jax.ShapeDtypeStruct((total, rows, HD), jnp.bfloat16),
        compiler_params=pltpu.CompilerParams(
            dimension_semantics=("arbitrary",), vmem_limit_bytes=52 << 20
        ),
        cost_estimate=pl.CostEstimate(
            flops=8 * total * rows * HD,
            bytes_accessed=10 * total * rows * HD,
            transcendentals=0,
        ),
    )(*arrays)


def combine_kernel(holders, x_ref, own_ref, value_ref, o_ref, w_ref):
    users = value_ref.shape[0]
    low = lax.broadcasted_iota(jnp.int32, (1, HD), 1) < ROWS
    for u in range(users):
        own = own_ref[u]
        senders = [i for i, w in enumerate(holders) if w == u]
        pairs = [stats_of(x_ref[i, ROWS:, :].astype(jnp.float32), low) for i in senders]
        peak = own
        for top, _ in pairs:
            peak = jnp.maximum(peak, top)
        fresh = jnp.exp2(own - peak)
        total = fresh
        for i, (top, mass) in zip(senders, pairs):
            weight = mass * jnp.exp2(top - peak)
            w_ref[i : i + 1, :] = weight
            total = total + weight
        inverse = 1.0 / total
        acc = value_ref[u] * fresh
        for i in senders:
            acc = acc + x_ref[i, :ROWS, :].astype(jnp.float32) * w_ref[i : i + 1, :]
        turned = (acc * inverse).T
        o_ref[u] = jnp.concatenate([turned[:ROWS], turned[ROWS:]], axis=1).astype(
            jnp.bfloat16
        )


def combined(holders, x, own, value):
    users = value.shape[0]
    return pl.pallas_call(
        functools.partial(combine_kernel, holders),
        out_shape=jax.ShapeDtypeStruct((users, ROWS, HD), jnp.bfloat16),
        scratch_shapes=[pltpu.VMEM((x.shape[0], HD), jnp.float32)],
        compiler_params=pltpu.CompilerParams(vmem_limit_bytes=24 << 20),
        cost_estimate=pl.CostEstimate(
            flops=2 * x.size, bytes_accessed=2 * x.size, transcendentals=0
        ),
    )(x, own, value)


def moved(array, axis, step):
    if axis == "z":
        at = [(z % 2) * 2 + z // 2 for z in range(4)]
        pairs = [(at[z], at[(z + step) % 4]) for z in range(4)]
        return lax.ppermute(array, ("zl", "zh"), pairs)
    count = SIZES[FINE.index(axis)]
    return lax.ppermute(array, axis, [(i, (i + step) % count) for i in range(count)])


def body(queries, key_cache, value_cache, key_table, value_table, lengths, token_ids):
    users, beams, _ = queries.shape
    half = users // 2
    length = key_cache.shape[1]
    x, y, zl, zh, c = (lax.axis_index(n) for n in ("x", "y", "zl", "zh", "c"))
    row = (zl * SIZES[1] + y) * 2 + c
    col = x * SIZES[4] + zh
    swap = functools.partial(lax.ppermute, axis_name="c", perm=[(0, 1), (1, 0)])

    def halves(array):
        return (
            lax.dynamic_slice_in_dim(array, c * half, half, 0),
            lax.dynamic_slice_in_dim(array, (1 - c) * half, half, 0),
        )

    q = queries.reshape(users, beams, GROUP, HD).transpose(0, 2, 1, 3)
    q_mine, q_give = halves(q)
    t_mine, t_give = halves(token_ids)
    q_give, key_source = lax.optimization_barrier((q_give, key_cache))
    q_chip = jnp.concatenate([q_mine, swap(q_give)], axis=2).reshape(half, ROWS, HD)
    tokens = jnp.concatenate([t_mine, swap(t_give)], axis=1)

    holders = [
        (a + b + 2 * h + l) % half
        for l in range(SIZES[0])
        for b in range(SIZES[1])
        for a in range(SIZES[3])
        for h in range(SIZES[4])
    ]
    chips = len(holders)
    held = (x + y + 2 * zh + zl) % half
    marks = np.asarray(holders).reshape(chips, 1, 1)
    operand = jnp.broadcast_to(q_chip[0], (chips, ROWS, HD))
    for w in range(1, half):
        operand = jnp.where(marks == w, q_chip[w], operand)
    operand, value_source = lax.optimization_barrier((operand, value_cache))
    got = lax.all_to_all(operand, CHIPS, 0, 0, tiled=True)
    got = got.reshape(chips // KH, KH, ROWS, HD)

    k_other = swap(halves(key_source)[1])
    v_other = swap(halves(value_source)[1])
    got, k_other, v_other = lax.optimization_barrier((got, k_other, v_other))

    offset = (row * KH + col) * length
    other = ((row + 1 - 2 * c) * KH + col) * length

    info = jnp.stack([c * half, held, offset, other]).astype(jnp.int32)

    caches = (key_cache, k_other, value_cache, v_other)
    lead = got.shape[0] // 2
    computed = functools.partial(partials, info=info, lengths=lengths, caches=caches)

    def flat(parts):
        return [p.reshape(-1, ROWS + META, HD) for p in parts]

    ask1 = [moved(got[:lead], "x", 1), moved(got[lead:], "y", 1)]
    ask3 = [moved(got[:lead], "x", -1), moved(got[lead:], "y", -1)]
    ask2 = [moved(got, "z", 2)]
    begun = computed(0, asked=[got], parts=(0, PARTS // 2))
    ask1, ask3, begun = lax.optimization_barrier((ask1, ask3, begun))
    near, far = flat(computed(1, asked=ask1, results=2))
    back = [[moved(near, "x", -1), moved(far, "y", -1)]]
    ask3, _ = lax.optimization_barrier((ask3, near))
    near, far = flat(computed(-1, asked=ask3, results=2))
    back.append([moved(near, "x", 1), moved(far, "y", 1)])
    ask2, _, back[0] = lax.optimization_barrier((ask2, near, back[0]))
    near, far = flat(computed(2, asked=ask2, results=2))
    back.append([moved(near, "x", -2), moved(far, "z", -2)])
    begun, _ = lax.optimization_barrier((begun, near))
    back.append(
        flat(computed(0, asked=[got], parts=(PARTS // 2, PARTS - PARTS // 2), into=begun))
    )
    arrived = lax.all_to_all(merged(back), CHIPS, 0, 0, tiled=True)

    codes = jnp.arange(key_table.shape[0], dtype=jnp.int32)
    onehot = (tokens[..., None] == codes).astype(jnp.bfloat16)
    keys = lax.dynamic_slice_in_dim(key_table, col * HD, HD, 1)
    values = lax.dynamic_slice_in_dim(value_table, col * HD, HD, 1)
    own_keys = jnp.einsum("uwv,vc->uwc", onehot, keys, preferred_element_type=jnp.float32)
    own_values = jnp.einsum("uwv,vc->uwc", onehot, values, preferred_element_type=jnp.float32)
    q_rows = q_chip.reshape(half, GROUP, 2 * beams, HD).astype(jnp.float32)
    own = jnp.sum(q_rows * own_keys[:, None], axis=-1) * SCALE2
    own = jnp.tile(own.reshape(half, 1, ROWS), (1, 1, 2))
    own_values = own_values.reshape(half, 2 * beams, 2, HALF).transpose(0, 3, 2, 1)
    own_values = jnp.broadcast_to(
        own_values[:, :, :, None], (half, HALF, 2, GROUP, 2 * beams)
    ).reshape(half, HALF, HD)

    result = combined(holders, arrived, own, own_values)
    result = result.reshape(half, GROUP, 2 * beams, HD)
    kept = result[:, :, :beams]
    received = swap(result[:, :, beams:])
    whole = jnp.where(
        c == 0, jnp.concatenate([kept, received]), jnp.concatenate([received, kept])
    )
    return whole.transpose(0, 2, 1, 3).reshape(users, beams, GROUP * HD)


def solution(mesh):
    fine = Mesh(np.asarray(mesh.devices).reshape(SIZES), FINE)
    row, col = ("zl", "y", "c"), ("x", "zh")
    return jax.shard_map(
        body,
        mesh=fine,
        in_specs=(
            P(None, row, col),
            P(None, row + col, None),
            P(None, row + col, None),
            P(),
            P(),
            P(),
            P(None, row),
        ),
        out_specs=P(None, row, col),
        check_vma=False,
    )
```
